256 devices in a mesh: blk: 64 (over z_hi, y, x), dom: 4 (over z_lo, core).
Axes of the slice: x: 4, y: 4, z: 8 (z_hi: 4, z_lo: 2; z = z_hi * 2 + z_lo), core: 2. Of those that a mesh axis runs over, the one named last changes fastest.
Arguments:
- pno_basis: float32 [2048, 64, 256], P(('blk', 'dom')), may hold values from -0.375 to 0.375
- amplitudes: float32 [2048, 4096], P(('blk', 'dom')), may hold values from -6 to 6
- send_list: int32 [64, 4, 64, 1], P('blk', 'dom'), may hold values from 0 to 7
- couple: int32 [2048, 8], P(('blk', 'dom')), may hold values from 0 to 63, as said below
- couple_weight: float32 [2048, 8], P(('blk', 'dom')), may hold values from 0.25 to 1
- fit_weight: float32 [2048, 16], P(('blk', 'dom')), may hold values from 0.25 to 1
- fit_blocks: float32 [128, 2, 256, 256], P('blk', None, 'dom'), may hold values from -0.375 to 0.375
Outputs:
- updated: float32 [2048, 4096], P(('blk', 'dom'))
The draws below stay inside these ranges and needn't reach their ends.
Inputs may be any that keep to these rules, and one draw needn't show every extreme that they name: `couple`: slot j of a device holds what peer j // 1 of blk sent it in its place j % 1; on every device each slot is named by at least one coupling.
All inputs are finite; a program needn't handle non-finite values.
Results may differ from the reference program's by a relative error of at most 0.0003.
Values sent between devices are 32-bit elements; how exact they have to be, the bound alone decides.
A program may use at most 64 MiB of HBM per device.

```python
import math
import jax
import jax.numpy as jnp
from jax import lax

NORB = 256
NPNO = 64
PAIR_DEV = 8
NCPL = 8
CAP = 1
STOPS = 8
FB_DEV = 2
PAIRS = 2048
FBLOCKS = 128
N_BLK = 64
N_DOM = 4


def draw_couple(key, part):
    read_count = PAIR_DEV * NCPL
    slot_count = N_BLK * CAP
    owner_count = PAIRS // PAIR_DEV
    random_scores = jax.random.randint(key, (owner_count, read_count), 0, 1 << 20) * read_count + jnp.arange(read_count, dtype=jnp.int32)[None, :]
    ordering = jnp.argsort(random_scores, axis=1, stable=True).astype(jnp.int32)
    return (ordering % slot_count).reshape(PAIRS, NCPL)


def place_ends(drawn, key, least, top_value):
    extent = drawn.shape
    place = [jax.random.randint(jax.random.fold_in(key, axis), (), 0, extent[axis]) for axis in range(len(extent))]
    drawn = drawn.at[tuple(place)].set(least)
    longest = extent.index(max(extent))
    place[longest] = (place[longest] + 1) % extent[longest]
    return drawn.at[tuple(place)].set(top_value)


def steps_of(stream_key, extent, split, smallest, largest):
    factor_of, own = 1.0, jax.random.fold_in(stream_key, 6)
    for dim, parts in split:
        draws = jnp.exp(jax.random.uniform(jax.random.fold_in(own, dim), (parts,), jnp.float32, smallest / len(split), largest / len(split)))
        factor_of = factor_of * jnp.repeat(draws, extent[dim] // parts).reshape([-1 if axis == dim else 1 for axis in range(len(extent))])
    return factor_of


def scatter_about(key, shape, deviation, bound, pieces=(), kind=jnp.bfloat16):
    values = deviation * jax.random.normal(key, shape, jnp.float32)
    if pieces:
        values = values * steps_of(key, shape, pieces, -0.22, 0.18)
    return jnp.clip(values, -bound, bound).astype(kind)


def setup_inputs(seed: int = 0) -> dict:
    streams_of = jax.random.split(jax.random.key(seed), 8)
    pno_basis = scatter_about(streams_of[0], (PAIRS, NPNO, NORB), NORB ** -0.5, 0.375, ((0, 256),), jnp.float32)
    amplitudes = scatter_about(streams_of[1], (PAIRS, NPNO * NPNO), 1.0, 6.0, ((0, 256),), jnp.float32)
    send_list = place_ends(jax.random.randint(streams_of[2], (N_BLK, N_DOM, N_BLK, CAP), 0, PAIR_DEV), jax.random.fold_in(streams_of[2], 1), 0, PAIR_DEV - 1).astype(jnp.int32)
    couple = draw_couple(jax.random.fold_in(streams_of[7], 71), 0)
    couple_weight = jnp.clip(jnp.exp(math.log(1.0) - 1.3862944 * jax.random.uniform(streams_of[4], (PAIRS, NCPL), jnp.float32) ** steps_of(streams_of[4], (PAIRS, NCPL), ((0, 256),), -0.2, 0.2)), 0.25, 1.0)
    fit_weight = jnp.clip(jnp.exp(math.log(1.0) - 1.3862944 * jax.random.uniform(streams_of[5], (PAIRS, STOPS * FB_DEV), jnp.float32) ** steps_of(streams_of[5], (PAIRS, STOPS * FB_DEV), ((0, 256),), -0.2, 0.2)), 0.25, 1.0)
    fit_blocks = scatter_about(streams_of[6], (FBLOCKS, 2, NORB, NORB), NORB ** -0.5, 0.375, ((0, 64), (2, 4)), jnp.float32)
    return dict(pno_basis=pno_basis, amplitudes=amplitudes, send_list=send_list, couple=couple, couple_weight=couple_weight, fit_weight=fit_weight, fit_blocks=fit_blocks)


HIGHEST = lax.Precision.HIGHEST


def couple_term(pair_basis, pair_amps, partner_basis, partner_amps, weights):
    intersection = jnp.einsum('par,pcbr->pcab', pair_basis, partner_basis, precision=HIGHEST)
    half_product = jnp.einsum('pcab,pcbe->pcae', intersection, partner_amps, precision=HIGHEST)
    sandwich = jnp.einsum('pcae,pcfe->pcaf', half_product, intersection, precision=HIGHEST)
    return pair_amps + jnp.einsum('pc,pcaf->paf', weights, sandwich, precision=HIGHEST)


def fit_term(pair_basis, dressed, blocks, weights):
    pair_count, pno_count, orbital_count = pair_basis.shape
    flat_basis = pair_basis.reshape(pair_count * pno_count, orbital_count)
    stacked = blocks.reshape(2 * orbital_count, orbital_count)
    projected = jnp.dot(flat_basis, stacked.T, precision=HIGHEST, preferred_element_type=jnp.float32)
    projected = projected.reshape(pair_count, pno_count, 2, orbital_count)
    inner_blocks = jnp.einsum('par,pbmr->mpab', pair_basis, projected, precision=HIGHEST)
    left_product = jnp.einsum('pai,pij->paj', inner_blocks[0], dressed, precision=HIGHEST)
    fit_contrib = jnp.einsum('paj,pbj->pab', left_product, inner_blocks[1], precision=HIGHEST)
    return weights[:, None, None] * fit_contrib


def reference(pno_basis, amplitudes, send_list, couple, couple_weight, fit_weight, fit_blocks):
    pno_count = pno_basis.shape[1]
    group_size = PAIR_DEV * N_DOM
    all_amps = amplitudes.reshape(-1, pno_count, pno_count)

    def per_group(group_index):
        start = group_index * group_size
        pair_basis = lax.dynamic_slice_in_dim(pno_basis, start, group_size, 0)
        own_amps = lax.dynamic_slice_in_dim(all_amps, start, group_size, 0)
        coupled = lax.dynamic_slice_in_dim(couple, start, group_size, 0)
        coupling_weights = lax.dynamic_slice_in_dim(couple_weight, start, group_size, 0)
        fitting_weights = lax.dynamic_slice_in_dim(fit_weight, start, group_size, 0)
        domain_index = (jnp.arange(group_size, dtype=jnp.int32) // PAIR_DEV)[:, None]
        peer_index = coupled // CAP
        slot_index = coupled % CAP
        local_index = send_list[peer_index, domain_index, group_index, slot_index]
        partner = (peer_index * N_DOM + domain_index) * PAIR_DEV + local_index
        dressed = couple_term(pair_basis, own_amps, pno_basis[partner], all_amps[partner], coupling_weights)
        updated_amps = dressed
        for stop_index in range(STOPS):
            source = (group_index - stop_index) % N_BLK
            for block_index in range(FB_DEV):
                blocks = lax.dynamic_index_in_dim(fit_blocks, source * FB_DEV + block_index, 0, keepdims=False)
                updated_amps = updated_amps + fit_term(pair_basis, dressed, blocks, fitting_weights[:, stop_index * FB_DEV + block_index])
        return updated_amps.reshape(group_size, pno_count * pno_count)

    result = lax.map(per_group, jnp.arange(N_BLK, dtype=jnp.int32))
    return result.reshape(-1, pno_count * pno_count)
```

```python
import functools

import jax
import jax.numpy as jnp
from jax import lax
from jax.experimental import pallas as pl
from jax.experimental.pallas import tpu as pltpu
from jax.sharding import PartitionSpec as P

MESH = pl.DeviceIdType.MESH
BF, F32 = jnp.bfloat16, jnp.float32
PAIRS, PNO, ORB = 8, 64, 256
ROWS = PNO + 16
SLOTS = 64

SHARD, BASES, WEIGHTS, TABLE, Z1A, Z1B, Z3A, Z3B, RELAYA, RELAYB, FY, FX, CORE, DSEND, PSEND = (
    0, 1, 2, 2, 6, 7, 8, 9, 10, 11, 12, 12, 16, 20, 21,
)
TRANSFERS = 22
NN = (((1,), (0,)), ((), ()))
NT = (((1,), (1,)), ((), ()))


def split(v):
    high = v.astype(BF)
    return high, (v - high.astype(F32)).astype(BF)


def dot3(a, b, dims):
    one = functools.partial(lax.dot_general, dimension_numbers=dims, preferred_element_type=F32)
    return one(a[0], b[0]) + (one(a[0], b[1]) + one(a[1], b[0]))


def natural(a4):
    return jnp.concatenate([a4[:, PNO * u : PNO * (u + 1)] for u in range(4)], axis=0)


def place():
    blk, dom = lax.axis_index("blk"), lax.axis_index("dom")
    return lax.div(blk, 16), lax.rem(lax.div(blk, 4), 4), lax.rem(blk, 4), lax.div(dom, 2), lax.rem(dom, 2)


def device(zh, y, x, zl, core):
    return (lax.rem(zh, 4) * 4 + lax.rem(y, 4)) * 4 + lax.rem(x, 4), zl * 2 + core


def kernel(
    sends_ref, readers_ref, where_ref, scale_ref,
    packed, shard, weights, tables,
    out_ref,
    z1, z2, z3, tables_in, tables_sm, stage, arrived, whole, slots, partner_bases, partner_weights,
    basis_h, basis_l, other_h, other_l, block_h, block_l, proj_h, proj_l,
    f0_h, f0_l, f1_h, f1_l, terms, dressed, d_send, d_recv, part_send, part_recv,
    plane_send, plane_recv, send_sem, recv_sem, local_sem,
):
    zh, y, x, zl, core = place()
    partner = device(zh, y, x, 1 - zl, core)
    twin = device(zh, y, x, zl, 1 - core)
    up, down, across = (device(zh + k, y, x, zl, core) for k in (1, 3, 2))
    step_y = 2 - zl
    fit_to = device(zh + lax.div(y + step_y, 4), y + step_y, x, zl, core)
    fit_from = device(zh + 3 + lax.div(y + 4 - step_y, 4), y + 4 - step_y, x, zl, core)

    def across_plane(t):
        return device(zh, y + lax.div(t, 4), x + lax.rem(t, 4), zl, core)

    def copy(n, src, dst, to):
        return pltpu.make_async_remote_copy(
            src_ref=src, dst_ref=dst, send_sem=send_sem.at[n], recv_sem=recv_sem.at[n],
            device_id=to, device_id_type=MESH,
        )

    def plane_copy(dz, t):
        n = dz * 16 + t
        return pltpu.make_async_remote_copy(
            src_ref=stage.at[n], dst_ref=arrived.at[n], send_sem=plane_send.at[n], recv_sem=plane_recv.at[n],
            device_id=across_plane(t), device_id_type=MESH,
        )

    sh = copy(SHARD, shard, whole.at[0, zl], partner)
    bases = copy(BASES, packed.at[:, pl.ds(0, PNO), :], partner_bases, partner)
    wts = copy(WEIGHTS, weights.at[1], partner_weights, partner)
    tabs = {dz: copy(TABLE + dz, tables.at[dz], tables_in.at[dz], to) for dz, to in ((1, up), (2, across), (3, down))}
    low, high = pl.ds(0, 4), pl.ds(4, 4)
    z1a = copy(Z1A, packed.at[low], z1.at[low], up)
    z1b = copy(Z1B, packed.at[high], z1.at[high], up)
    z3a = copy(Z3A, packed.at[low], z3.at[low], down)
    z3b = copy(Z3B, packed.at[high], z3.at[high], down)
    relay_a = copy(RELAYA, z1.at[low], z2.at[low], up)
    relay_b = copy(RELAYB, z3.at[high], z2.at[high], down)
    fy = copy(FY, whole.at[0], whole.at[1], fit_to)

    def fx(dx, which):
        return copy(FX + dx, whole.at[which], slots.at[dx, :, core], device(zh, y, x + dx, zl, core))

    def to_twin(j):
        return copy(CORE + j, slots.at[j, :, core], slots.at[j, :, core], twin)

    def first_slot(which):
        pltpu.make_async_copy(whole.at[which], slots.at[0, :, core], local_sem.at[1]).start()
        copy(CORE, whole.at[which], slots.at[0, :, core], twin).start()

    def fill_stage(source, index_of, dz):
        arrived[dz * 16] = source[index_of(0)]

        def one(t, _):
            stage[dz * 16 + t] = source[index_of(t)]
            return 0

        lax.fori_loop(1, 16, one, 0)

    def send_stage(dz):
        def one(t, _):
            plane_copy(dz, t).start()
            return 0

        lax.fori_loop(1, 16, one, 0)

    barrier = pltpu.get_barrier_semaphore()

    def greet(to):
        pl.semaphore_signal(barrier, inc=1, device_id=to, device_id_type=MESH)

    def greet_plane(t, _):
        greet(across_plane(t))
        return 0

    lax.fori_loop(1, 16, greet_plane, 0)
    for to in (partner, twin, up, down, across, fit_to, fit_from):
        greet(to)
    own_shard = pltpu.make_async_copy(shard, whole.at[0, zl], local_sem.at[0])
    own_shard.start()
    fill_stage(packed, lambda t: sends_ref[t], 0)

    def split_own(p, _):
        basis_h[p], basis_l[p] = split(packed[p, :PNO, :])
        return 0

    lax.fori_loop(0, PAIRS, split_own, 0)
    own_shard.wait()
    pl.semaphore_wait(barrier, 22)

    sh.start()
    for dz in (1, 3, 2):
        tabs[dz].start()
    z1a.start()
    z3b.start()
    send_stage(0)
    z1b.start()
    z3a.start()
    wts.start()
    bases.start()

    sh.wait_recv()
    fy.start()

    @pl.when(zl == 0)
    def _():
        first_slot(0)

    def own_rows(dx):
        return (1 - zl) * (1 - lax.div(x + dx, 4))

    for dx in (1, 3, 2):

        @pl.when(own_rows(dx) == 1)
        def _():
            fx(dx, 0).start()

    z1a.wait_recv()
    relay_a.start()
    z3b.wait_recv()
    relay_b.start()
    fy.wait_recv()
    for dx in (1, 3, 2):

        @pl.when(own_rows(dx) == 0)
        def _():
            fx(dx, 1).start()

    @pl.when(zl == 1)
    def _():
        first_slot(1)

    def pass_on(dz, source):
        tabs[dz].wait_recv()
        table = pltpu.make_async_copy(tables_in.at[dz], tables_sm.at[dz], local_sem.at[1 + dz])
        table.start()
        table.wait()
        fill_stage(source, lambda t: tables_sm[dz, 0, t], dz)
        send_stage(dz)

    def dress(dz):
        def one_of(t):
            return pltpu.make_async_remote_copy(
                src_ref=stage.at[t], dst_ref=arrived.at[t], send_sem=plane_send.at[t], recv_sem=plane_recv.at[t],
                device_id=twin, device_id_type=MESH,
            )

        def arrive(t, _):
            one_of(t).wait_recv()
            return 0

        lax.fori_loop(dz * 16 + 1, dz * 16 + 16, arrive, 0)

        def some(i, _):
            for u in range(4):
                t = dz * 16 + i * 4 + u
                reader = readers_ref[t]
                own = basis_h[reader], basis_l[reader]
                overlap = split(dot3(own, split(arrived[t, :PNO, :]), NT))
                half = split(dot3(overlap, split(natural(arrived[t, PNO:, :])), NN))
                terms[t] = scale_ref[t] * dot3(half, overlap, NT)
            return 0

        lax.fori_loop(0, 4, some, 0)

    def fit(j, group):
        bases_h, bases_l = (basis_h, basis_l) if group == 0 else (other_h, other_l)
        rows_of = weights.at[0] if group == 0 else partner_weights

        def project(n, _):
            flat = (bases_h[...].reshape(PAIRS * PNO, ORB), bases_l[...].reshape(PAIRS * PNO, ORB))
            proj_h[n], proj_l[n] = split(dot3(flat, (block_h[n], block_l[n]), NN))
            return 0

        lax.fori_loop(0, 4, project, 0)

        def pair(p, _):
            rows = pl.ds(pl.multiple_of(p * PNO, PNO), PNO)
            left = proj_h[:, rows, :].reshape(4 * PNO, ORB), proj_l[:, rows, :].reshape(4 * PNO, ORB)
            both = dot3(left, (bases_h[p], bases_l[p]), NT)
            n = group * PAIRS + p
            for k in range(2):
                weight = rows_of[pl.ds(p * 8 + j * 2 + k, 1), :][:, :PNO]
                to = pl.ds((j * 2 + k) * PNO, PNO)
                f0_h[n, to, :], f0_l[n, to, :] = split(both[k * PNO : (k + 1) * PNO] * weight)
                f1_h[n, to, :], f1_l[n, to, :] = split(both[(2 + k) * PNO : (3 + k) * PNO])
            return 0

        lax.fori_loop(0, PAIRS, pair, 0)

    def load_blocks(j):
        for n in range(4):
            m, k = n // 2, n % 2
            rows = [slots[j, a, b, k, m] for a in range(2) for b in range(2)]
            block_h[n], block_l[n] = split(jnp.concatenate(rows, axis=0))

    z1b.wait_recv()
    pass_on(1, z1)
    z3a.wait_recv()
    pass_on(3, z3)
    dress(0)
    to_twin(0).wait_recv()
    pltpu.make_async_copy(whole.at[0], slots.at[0, :, core], local_sem.at[1]).wait()
    load_blocks(0)
    fit(0, 0)
    relay_a.wait_recv()
    relay_b.wait_recv()
    pass_on(2, z2)
    for dx in (1, 3, 2):
        fx(dx, 0).wait_recv()
        to_twin(dx).start()
    wts.wait_recv()
    bases.wait_recv()

    def split_other(p, _):
        other_h[p], other_l[p] = split(partner_bases[p])
        return 0

    lax.fori_loop(0, PAIRS, split_other, 0)
    fit(0, 1)
    dress(1)
    dress(3)
    for j in (1, 3, 2):
        to_twin(j).wait_recv()
        load_blocks(j)
        fit(j, 0)
        fit(j, 1)
    dress(2)

    def gather_terms(p, _):
        total = natural(packed[p, PNO:, :])
        for c in range(8):
            total = total + terms[where_ref[p * 8 + c]]
        dressed[p] = total
        return 0

    lax.fori_loop(0, PAIRS, gather_terms, 0)
    for q in range(4):
        d_send[q] = jnp.concatenate([dressed[q], dressed[q + 4]], axis=1)
    ds = copy(DSEND, d_send, d_recv, partner)
    ds.start()

    def fitted_sum(n, d):
        left = dot3((f0_h[n], f0_l[n]), split(d), NN)
        left_h, left_l = split(left)
        total = jnp.zeros((PNO, PNO), F32)
        for i in range(8):
            r = slice(i * PNO, (i + 1) * PNO)
            total = total + dot3((left_h[r], left_l[r]), (f1_h[n, r, :], f1_l[n, r, :]), NT)
        return total

    def finish_own(p, _):
        dressed[p] = dressed[p] + fitted_sum(p, dressed[p])
        return 0

    lax.fori_loop(0, PAIRS, finish_own, 0)
    ds.wait_recv()

    def finish_other(q, _):
        two = d_recv[q]
        part_send[q] = jnp.concatenate(
            [fitted_sum(PAIRS + q, two[:, :PNO]), fitted_sum(PAIRS + q + 4, two[:, PNO:])], axis=1
        )
        return 0

    lax.fori_loop(0, 4, finish_other, 0)
    ps = copy(PSEND, part_send, part_recv, partner)
    ps.start()

    for done in (sh, bases, wts, z1a, z1b, z3a, z3b, relay_a, relay_b, fy, ds, *tabs.values()):
        done.wait_send()
    for dx in (1, 2, 3):
        fx(dx, 0).wait_send()
    for j in range(4):
        to_twin(j).wait_send()

    def plane_sent(n, _):
        @pl.when(lax.rem(n, 16) > 0)
        def _():
            plane_copy(lax.div(n, 16), lax.rem(n, 16)).wait_send()

        return 0

    lax.fori_loop(0, SLOTS, plane_sent, 0)
    ps.wait()
    for q in range(4):
        two = part_recv[q]
        out_ref[q] = dressed[q] + two[:, :PNO]
        out_ref[q + 4] = dressed[q + 4] + two[:, PNO:]


def on_device(pno_basis, amplitudes, send_list, couple, couple_weight, fit_weight, fit_blocks):
    zh, y, x, zl, _ = place()
    quarters = amplitudes.reshape(PAIRS, 4, 16, PNO).transpose(0, 2, 1, 3).reshape(PAIRS, 16, ORB)
    packed = jnp.concatenate([pno_basis, quarters], axis=1)

    t = jnp.arange(SLOTS, dtype=jnp.int32)
    dz, dy, dx = t // 16, (t // 4) % 4, t % 4
    source = ((zh + 4 - dz) % 4) * 16 + ((y + 4 - dy) % 4) * 4 + (x + 4 - dx) % 4
    reads = couple.reshape(1, -1) == source[:, None]
    readers = jnp.sum(jnp.where(reads, t[None, :] // 8, 0), axis=1)
    scale = jnp.sum(jnp.where(reads, couple_weight.reshape(1, -1), 0.0), axis=1)
    where = jnp.sum(jnp.where(reads, t[:, None], 0), axis=0)
    target = ((zh + dz) % 4) * 16 + ((y + dy) % 4) * 4 + (x + dx) % 4
    sends = jnp.sum(jnp.where(target[:, None] == t[None, :], send_list.reshape(1, -1), 0), axis=1)
    tables = jnp.broadcast_to(jnp.pad(sends.reshape(4, 1, 16), ((0, 0), (0, 0), (0, 112))), (4, 8, 128))

    j = jnp.arange(8, dtype=jnp.int32) // 2
    bit = jnp.arange(8, dtype=jnp.int32) % 2
    late = jnp.where(x < j, 1, 0)
    stop_even, stop_odd = j + 4 * late, j + 4 * (1 - late)
    stops = jnp.stack([jnp.where(zl == 0, stop_even, stop_odd), jnp.where(zl == 0, stop_odd, stop_even)])
    column = stops * 2 + bit
    chosen = jnp.sum(
        jnp.where(column[:, None, :, None] == jnp.arange(16)[None, None, None, :], fit_weight[None, :, None, :], 0.0), axis=3
    )
    weights = jnp.broadcast_to(chosen.reshape(2, SLOTS, 1), (2, SLOTS, 128))

    vmem, smem = pl.BlockSpec(memory_space=pltpu.VMEM), pl.BlockSpec(memory_space=pltpu.SMEM)
    tile = functools.partial(pltpu.VMEM, dtype=F32)
    narrow = functools.partial(pltpu.VMEM, dtype=BF)
    out = pl.pallas_call(
        kernel,
        out_shape=jax.ShapeDtypeStruct((PAIRS, PNO, PNO), F32),
        in_specs=[smem] * 4 + [vmem] * 4,
        out_specs=vmem,
        scratch_shapes=[
            tile((PAIRS, ROWS, ORB)), tile((PAIRS, ROWS, ORB)), tile((PAIRS, ROWS, ORB)),
            pltpu.VMEM((4, 8, 128), jnp.int32), pltpu.SMEM((4, 8, 128), jnp.int32),
            tile((SLOTS, ROWS, ORB)), tile((SLOTS, ROWS, ORB)),
            tile((2, 2, 2, 2, PNO, ORB)), tile((4, 2, 2, 2, 2, PNO, ORB)),
            tile((PAIRS, PNO, ORB)), tile((SLOTS, 128)),
            narrow((PAIRS, PNO, ORB)), narrow((PAIRS, PNO, ORB)), narrow((PAIRS, PNO, ORB)), narrow((PAIRS, PNO, ORB)),
            narrow((4, ORB, ORB)), narrow((4, ORB, ORB)),
            narrow((4, PAIRS * PNO, ORB)), narrow((4, PAIRS * PNO, ORB)),
            narrow((16, 512, PNO)), narrow((16, 512, PNO)), narrow((16, 512, PNO)), narrow((16, 512, PNO)),
            tile((SLOTS, PNO, PNO)), tile((PAIRS, PNO, PNO)),
            tile((4, PNO, 128)), tile((4, PNO, 128)), tile((4, PNO, 128)), tile((4, PNO, 128)),
            pltpu.SemaphoreType.DMA((SLOTS,)), pltpu.SemaphoreType.DMA((SLOTS,)),
            pltpu.SemaphoreType.DMA((TRANSFERS,)), pltpu.SemaphoreType.DMA((TRANSFERS,)),
            pltpu.SemaphoreType.DMA((5,)),
        ],
        compiler_params=pltpu.CompilerParams(
            collective_id=0, has_side_effects=True, vmem_limit_bytes=60 * 1024 * 1024
        ),
    )(sends[:16], readers, where, scale, packed, fit_blocks, weights, tables)
    return out.reshape(PAIRS, PNO * PNO)


def solution(mesh):
    placed = (
        P(("blk", "dom"), None, None),
        P(("blk", "dom"), None),
        P("blk", "dom", None, None),
        P(("blk", "dom"), None),
        P(("blk", "dom"), None),
        P(("blk", "dom"), None),
        P("blk", None, "dom", None),
    )
    return jax.shard_map(
        on_device, mesh=mesh, in_specs=placed, out_specs=P(("blk", "dom"), None), check_vma=False
    )
```

```python
import functools

import jax
import jax.numpy as jnp
from jax import lax
from jax.experimental import pallas as pl
from jax.experimental.pallas import tpu as pltpu
from jax.sharding import PartitionSpec as P

MESH = pl.DeviceIdType.MESH
BF, F32 = jnp.bfloat16, jnp.float32
PAIRS, PNO, ORB = 8, 64, 256
ROWS = PNO + 16
SLOTS = 64

SHARD, BASES, WEIGHTS, TABLE, DSEND, PSEND, FY, CORE, UP, DOWN, RELAY, FX = (
    0, 1, 2, 2, 6, 7, 8, 16, 20, 28, 36, 40,
)
TRANSFERS = 56
NN = (((1,), (0,)), ((), ()))
NT = (((1,), (1,)), ((), ()))


def split(v):
    high = v.astype(BF)
    return high, (v - high.astype(F32)).astype(BF)


def dot3(a, b, dims):
    one = functools.partial(lax.dot_general, dimension_numbers=dims, preferred_element_type=F32)
    return one(a[0], b[0]) + (one(a[0], b[1]) + one(a[1], b[0]))


def natural(a4):
    return jnp.concatenate([a4[:, PNO * u : PNO * (u + 1)] for u in range(4)], axis=0)


def place():
    blk, dom = lax.axis_index("blk"), lax.axis_index("dom")
    return lax.div(blk, 16), lax.rem(lax.div(blk, 4), 4), lax.rem(blk, 4), lax.div(dom, 2), lax.rem(dom, 2)


def device(zh, y, x, zl, core):
    return (lax.rem(zh, 4) * 4 + lax.rem(y, 4)) * 4 + lax.rem(x, 4), zl * 2 + core


def kernel(
    sends_ref, inverse_ref, couple_ref, scale_ref, rate_ref,
    packed, shard, weights, table,
    out_ref,
    z1, z2, z3, tables_in, tables_sm, stage, arrived, whole, slots, partner_bases, partner_weights, partner_rates,
    basis_h, basis_l, other_h, other_l, block_h, block_l, proj_h, proj_l,
    f0_h, f0_l, f1_h, f1_l, terms, dressed, d_send, d_recv, part_send, part_recv,
    plane_send, plane_recv, send_sem, recv_sem, local_sem,
):
    zh, y, x, zl, core = place()
    partner = device(zh, y, x, 1 - zl, core)
    twin = device(zh, y, x, zl, 1 - core)
    up, down, across = (device(zh + k, y, x, zl, core) for k in (1, 3, 2))
    step_y = 2 - zl
    fit_to = device(zh + lax.div(y + step_y, 4), y + step_y, x, zl, core)
    fit_from = device(zh + 3 + lax.div(y + 4 - step_y, 4), y + 4 - step_y, x, zl, core)

    def across_plane(t):
        return device(zh, y + lax.div(t, 4), x + lax.rem(t, 4), zl, core)

    def copy(n, src, dst, to):
        return pltpu.make_async_remote_copy(
            src_ref=src, dst_ref=dst, send_sem=send_sem.at[n], recv_sem=recv_sem.at[n],
            device_id=to, device_id_type=MESH,
        )

    def plane_copy(dz, t):
        n = dz * 16 + t
        return pltpu.make_async_remote_copy(
            src_ref=stage.at[n], dst_ref=arrived.at[n], send_sem=plane_send.at[n], recv_sem=plane_recv.at[n],
            device_id=across_plane(t), device_id_type=MESH,
        )

    sh = copy(SHARD, shard, whole.at[0, zl], partner)
    bases = copy(BASES, packed.at[:, pl.ds(0, PNO), :], partner_bases, partner)
    wts = copy(WEIGHTS, weights, partner_weights, partner)
    tabs = {dz: copy(TABLE + dz, table, tables_in.at[dz], to) for dz, to in ((1, up), (2, across), (3, down))}

    def z_up(i):
        return copy(UP + i, packed.at[i], z1.at[i], up)

    def z_down(i):
        return copy(DOWN + i, packed.at[i], z3.at[i], down)

    def relay(i):
        if i < 4:
            return copy(RELAY + i, z1.at[i], z2.at[i], up)
        return copy(RELAY + i, z3.at[i], z2.at[i], down)

    def fy(a):
        return copy(FY + a, whole.at[0, a], whole.at[1, a], fit_to)


    def fx(dx, which, i):
        a, k = i // 2, i % 2
        return copy(
            FX + dx * 4 + i, whole.at[which, a, k], slots.at[dx, a, core, k], device(zh, y, x + dx, zl, core)
        )

    def send_rows(which, pieces):
        for i in pieces:
            for dx in (1, 3, 2):

                @pl.when(own_rows(dx) == 1 - which)
                def _():
                    fx(dx, which, i).start()

    def to_twin(j):
        return copy(CORE + j, slots.at[j, :, core], slots.at[j, :, core], twin)

    def first_slot(which):
        pltpu.make_async_copy(whole.at[which], slots.at[0, :, core], local_sem.at[1]).start()
        copy(CORE, whole.at[which], slots.at[0, :, core], twin).start()

    def reader_of(t):
        return (zh * 4 + lax.rem(y + lax.div(t, 4), 4)) * 4 + lax.rem(x + lax.rem(t, 4), 4)

    def fill_stage(source, index_of, dz):
        arrived[dz * 16] = source[index_of(0)]

        def one(t, _):
            stage[dz * 16 + t] = source[index_of(t)]
            return 0

        lax.fori_loop(1, 16, one, 0)

    def send_stage(dz):
        for t in (1, 4, 3, 12, 5, 7, 13, 15, 2, 8, 6, 9, 14, 11, 10):
            plane_copy(dz, t).start()

    barrier = pltpu.get_barrier_semaphore()

    def greet(to):
        pl.semaphore_signal(barrier, inc=1, device_id=to, device_id_type=MESH)

    def greet_plane(t, _):
        greet(across_plane(t))
        return 0

    lax.fori_loop(1, 16, greet_plane, 0)
    for to in (partner, twin, up, down, across, fit_to, fit_from):
        greet(to)
    own_shard = pltpu.make_async_copy(shard, whole.at[0, zl], local_sem.at[0])
    own_shard.start()
    fill_stage(packed, lambda t: sends_ref[reader_of(t)], 0)

    def split_own(p, _):
        basis_h[p], basis_l[p] = split(packed[p, :PNO, :])
        return 0

    lax.fori_loop(0, PAIRS, split_own, 0)
    own_shard.wait()
    pl.semaphore_wait(barrier, 22)

    sh.start()
    for t in (1, 4, 3, 12, 5, 7, 13, 15):
        plane_copy(0, t).start()

    sh.wait_recv()
    fy(0).start()
    fy(1).start()
    for dz in (1, 3, 2):
        tabs[dz].start()
    for i in range(4):
        z_up(i).start()
        z_down(4 + i).start()
    for t in (2, 8, 6, 9, 14, 11, 10):
        plane_copy(0, t).start()

    @pl.when(zl == 0)
    def _():
        first_slot(0)

    def own_rows(dx):
        return (1 - zl) * (1 - lax.div(x + dx, 4))

    for i in range(4):
        z_up(4 + i).start()
        z_down(i).start()
        send_rows(0, (i,))
    fy(0).wait_recv()
    fy(1).wait_recv()
    for i in range(4):
        z_up(i).wait_recv()
        relay(i).start()
        z_down(4 + i).wait_recv()
        relay(4 + i).start()
        send_rows(1, (i,))

    @pl.when(zl == 1)
    def _():
        first_slot(1)

    def pass_on(dz, source):
        tabs[dz].wait_recv()
        table = pltpu.make_async_copy(tables_in.at[dz], tables_sm.at[dz], local_sem.at[1 + dz])
        table.start()
        table.wait()
        fill_stage(source, lambda t: tables_sm[dz, 0, reader_of(t)], dz)
        send_stage(dz)

    def dress(dz):
        def one_of(t):
            return pltpu.make_async_remote_copy(
                src_ref=stage.at[t], dst_ref=arrived.at[t], send_sem=plane_send.at[t], recv_sem=plane_recv.at[t],
                device_id=twin, device_id_type=MESH,
            )

        def arrive(t, _):
            one_of(t).wait_recv()
            return 0

        lax.fori_loop(dz * 16 + 1, dz * 16 + 16, arrive, 0)

        def some(i, _):
            for u in range(4):
                t = dz * 16 + i * 4 + u
                term = inverse_ref[t]
                reader, of = lax.div(term, 8), lax.rem(term, 8)
                own = basis_h[reader], basis_l[reader]
                overlap = split(dot3(own, split(arrived[t, :PNO, :]), NT))
                half = split(dot3(overlap, split(natural(arrived[t, PNO:, :])), NN))
                terms[t] = scale_ref[reader, of] * dot3(half, overlap, NT)
            return 0

        lax.fori_loop(0, 4, some, 0)

    def fit(j, group):
        bases_h, bases_l = (basis_h, basis_l) if group == 0 else (other_h, other_l)
        rates = rate_ref if group == 0 else partner_rates
        late = lax.div(3 - x + j, 4)
        stop = j + 4 * (zl + late - 2 * zl * late)

        def project(n, _):
            flat = (bases_h[...].reshape(PAIRS * PNO, ORB), bases_l[...].reshape(PAIRS * PNO, ORB))
            proj_h[n], proj_l[n] = split(dot3(flat, (block_h[n], block_l[n]), NN))
            return 0

        lax.fori_loop(0, 4, project, 0)

        def pair(p, _):
            rows = pl.ds(pl.multiple_of(p * PNO, PNO), PNO)
            left = proj_h[:, rows, :].reshape(4 * PNO, ORB), proj_l[:, rows, :].reshape(4 * PNO, ORB)
            both = dot3(left, (bases_h[p], bases_l[p]), NT)
            n = group * PAIRS + p
            for k in range(2):
                to = pl.ds((j * 2 + k) * PNO, PNO)
                f0_h[n, to, :], f0_l[n, to, :] = split(both[k * PNO : (k + 1) * PNO] * rates[p, stop * 2 + k])
            right = jnp.concatenate([both[2 * PNO : 3 * PNO], both[3 * PNO :]], axis=1)
            f1_h[n, :, pl.ds(j * 128, 128)], f1_l[n, :, pl.ds(j * 128, 128)] = split(right)
            return 0

        lax.fori_loop(0, PAIRS, pair, 0)

    def load_blocks(j):
        for n in range(4):
            m, k = n // 2, n % 2
            rows = [slots[j, a, b, k, m] for a in range(2) for b in range(2)]
            block_h[n], block_l[n] = split(jnp.concatenate(rows, axis=0))

    for i in range(4):
        z_up(4 + i).wait_recv()
    pass_on(1, z1)
    for i in range(4):
        z_down(i).wait_recv()
    pass_on(3, z3)
    wts.start()
    bases.start()
    dress(0)
    to_twin(0).wait_recv()
    pltpu.make_async_copy(whole.at[0], slots.at[0, :, core], local_sem.at[1]).wait()
    load_blocks(0)
    fit(0, 0)
    for i in range(8):
        relay(i).wait_recv()
    pass_on(2, z2)
    for dx in (1, 3, 2):
        for i in range(4):
            fx(dx, 0, i).wait_recv()
        to_twin(dx).start()
    wts.wait_recv()
    rates_in = pltpu.make_async_copy(partner_weights, partner_rates, local_sem.at[1])
    rates_in.start()
    bases.wait_recv()
    rates_in.wait()

    def split_other(p, _):
        other_h[p], other_l[p] = split(partner_bases[p])
        return 0

    lax.fori_loop(0, PAIRS, split_other, 0)
    fit(0, 1)
    dress(1)
    dress(3)
    for j in (1, 3, 2):
        to_twin(j).wait_recv()
        load_blocks(j)
        fit(j, 0)
        fit(j, 1)
    dress(2)

    def gather_terms(p, _):
        total = natural(packed[p, PNO:, :])
        for c in range(8):
            slot = couple_ref[p, c]
            back = lax.rem(zh + 4 - lax.div(slot, 16), 4) * 16 + lax.rem(y + 4 - lax.rem(lax.div(slot, 4), 4), 4) * 4
            total = total + terms[back + lax.rem(x + 4 - lax.rem(slot, 4), 4)]
        dressed[p] = total
        return 0

    lax.fori_loop(0, PAIRS, gather_terms, 0)
    for q in range(4):
        d_send[q] = jnp.concatenate([dressed[q], dressed[q + 4]], axis=1)
    ds = copy(DSEND, d_send, d_recv, partner)
    ds.start()

    def fitted_sum(n, d):
        left = dot3((f0_h[n], f0_l[n]), split(d), NN)
        left = jnp.concatenate(
            [jnp.concatenate([left[i * PNO : (i + 1) * PNO], left[(i + 1) * PNO : (i + 2) * PNO]], axis=1) for i in (0, 2, 4, 6)],
            axis=1,
        )
        return dot3(split(left), (f1_h[n], f1_l[n]), NT)

    def finish_own(p, _):
        dressed[p] = dressed[p] + fitted_sum(p, dressed[p])
        return 0

    lax.fori_loop(0, PAIRS, finish_own, 0)
    ds.wait_recv()

    def finish_other(q, _):
        two = d_recv[q]
        part_send[q] = jnp.concatenate(
            [fitted_sum(PAIRS + q, two[:, :PNO]), fitted_sum(PAIRS + q + 4, two[:, PNO:])], axis=1
        )
        return 0

    lax.fori_loop(0, 4, finish_other, 0)
    ps = copy(PSEND, part_send, part_recv, partner)
    ps.start()

    for done in (sh, bases, wts, fy(0), fy(1), ds, *tabs.values()):
        done.wait_send()
    for i in range(8):
        z_up(i).wait_send()
        z_down(i).wait_send()
        relay(i).wait_send()
    for dx in (1, 2, 3):
        for i in range(4):
            fx(dx, 0, i).wait_send()
    for j in range(4):
        to_twin(j).wait_send()

    def plane_sent(n, _):
        @pl.when(lax.rem(n, 16) > 0)
        def _():
            plane_copy(lax.div(n, 16), lax.rem(n, 16)).wait_send()

        return 0

    lax.fori_loop(0, SLOTS, plane_sent, 0)
    ps.wait()
    for q in range(4):
        two = part_recv[q]
        out_ref[q] = dressed[q] + two[:, :PNO]
        out_ref[q + 4] = dressed[q + 4] + two[:, PNO:]


def on_device(pno_basis, amplitudes, send_list, couple, couple_weight, fit_weight, fit_blocks):
    zh, y, x, zl, _ = place()
    quarters = amplitudes.reshape(PAIRS, 4, 16, PNO).transpose(0, 2, 1, 3).reshape(PAIRS, 16, ORB)
    packed = jnp.concatenate([pno_basis, quarters], axis=1)

    t = jnp.arange(SLOTS, dtype=jnp.int32)
    source = ((zh + 4 - t // 16) % 4) * 16 + ((y + 4 - (t // 4) % 4) % 4) * 4 + (x + 4 - t % 4) % 4
    term = jnp.arange(PAIRS, dtype=jnp.int32)[:, None] * 8 + jnp.arange(8, dtype=jnp.int32)[None, :]
    inverse = jnp.sum(jnp.where(couple[None] == source[:, None, None], term[None], 0), axis=(1, 2))
    sends = send_list.reshape(SLOTS)
    table = jnp.broadcast_to(jnp.pad(sends.reshape(1, SLOTS), ((0, 0), (0, 64))), (8, 128))
    weights = jnp.pad(fit_weight, ((0, 0), (0, 112)))

    vmem, smem = pl.BlockSpec(memory_space=pltpu.VMEM), pl.BlockSpec(memory_space=pltpu.SMEM)
    tile = functools.partial(pltpu.VMEM, dtype=F32)
    narrow = functools.partial(pltpu.VMEM, dtype=BF)
    out = pl.pallas_call(
        kernel,
        out_shape=jax.ShapeDtypeStruct((PAIRS, PNO, PNO), F32),
        in_specs=[smem] * 5 + [vmem] * 4,
        out_specs=vmem,
        scratch_shapes=[
            tile((PAIRS, ROWS, ORB)), tile((PAIRS, ROWS, ORB)), tile((PAIRS, ROWS, ORB)),
            pltpu.VMEM((4, 8, 128), jnp.int32), pltpu.SMEM((4, 8, 128), jnp.int32),
            tile((SLOTS, ROWS, ORB)), tile((SLOTS, ROWS, ORB)),
            tile((2, 2, 2, 2, PNO, ORB)), tile((4, 2, 2, 2, 2, PNO, ORB)),
            tile((PAIRS, PNO, ORB)), tile((PAIRS, 128)), pltpu.SMEM((PAIRS, 128), F32),
            narrow((PAIRS, PNO, ORB)), narrow((PAIRS, PNO, ORB)), narrow((PAIRS, PNO, ORB)), narrow((PAIRS, PNO, ORB)),
            narrow((4, ORB, ORB)), narrow((4, ORB, ORB)),
            narrow((4, PAIRS * PNO, ORB)), narrow((4, PAIRS * PNO, ORB)),
            narrow((16, 512, PNO)), narrow((16, 512, PNO)), narrow((16, PNO, 512)), narrow((16, PNO, 512)),
            tile((SLOTS, PNO, PNO)), tile((PAIRS, PNO, PNO)),
            tile((4, PNO, 128)), tile((4, PNO, 128)), tile((4, PNO, 128)), tile((4, PNO, 128)),
            pltpu.SemaphoreType.DMA((SLOTS,)), pltpu.SemaphoreType.DMA((SLOTS,)),
            pltpu.SemaphoreType.DMA((TRANSFERS,)), pltpu.SemaphoreType.DMA((TRANSFERS,)),
            pltpu.SemaphoreType.DMA((5,)),
        ],
        compiler_params=pltpu.CompilerParams(
            collective_id=0, has_side_effects=True, vmem_limit_bytes=60 * 1024 * 1024
        ),
    )(sends, inverse, couple, couple_weight, fit_weight, packed, fit_blocks, weights, table)
    return out.reshape(PAIRS, PNO * PNO)


def solution(mesh):
    placed = (
        P(("blk", "dom"), None, None),
        P(("blk", "dom"), None),
        P("blk", "dom", None, None),
        P(("blk", "dom"), None),
        P(("blk", "dom"), None),
        P(("blk", "dom"), None),
        P("blk", None, "dom", None),
    )
    return jax.shard_map(
        on_device, mesh=mesh, in_specs=placed, out_specs=P(("blk", "dom"), None), check_vma=False
    )
```

```python
import functools

import jax
import jax.numpy as jnp
from jax import lax
from jax.experimental import pallas as pl
from jax.experimental.pallas import tpu as pltpu
from jax.sharding import PartitionSpec as P

MESH = pl.DeviceIdType.MESH
BF, F32 = jnp.bfloat16, jnp.float32
PAIRS, PNO, ORB = 8, 64, 256
ROWS = PNO + 16
SLOTS = 64
SHIFT = 3

SHARD, BASES, WEIGHTS, TABLE, DSEND, PSEND, FY, CORE, UP, DOWN, RELAY, FX, DETOUR, ONWARD, SCALES, PARTS = (
    0, 1, 2, 2, 6, 7, 8, 16, 20, 28, 36, 40, 56, 58, 59, 62,
)
TRANSFERS = 66
NN = (((1,), (0,)), ((), ()))
NT = (((1,), (1,)), ((), ()))


def split(v):
    high = v.astype(BF)
    return high, (v - high.astype(F32)).astype(BF)


def dot3(a, b, dims):
    one = functools.partial(lax.dot_general, dimension_numbers=dims, preferred_element_type=F32)
    return one(a[0], b[0]) + (one(a[0], b[1]) + one(a[1], b[0]))


def natural(a4):
    return jnp.concatenate([a4[:, PNO * u : PNO * (u + 1)] for u in range(4)], axis=0)


def place():
    blk, dom = lax.axis_index("blk"), lax.axis_index("dom")
    return lax.div(blk, 16), lax.rem(lax.div(blk, 4), 4), lax.rem(blk, 4), lax.div(dom, 2), lax.rem(dom, 2)


def device(zh, y, x, zl, core):
    return (lax.rem(zh, 4) * 4 + lax.rem(y, 4)) * 4 + lax.rem(x, 4), zl * 2 + core


def kernel(
    sends_ref, inverse_ref, couple_ref, scale_ref, rate_ref,
    packed, shard, weights, table, scales,
    out_ref,
    z1, z2, z3, detour, tables_in, tables_sm, scales_in, scales_sm, z_send, z_part, stage, arrived, whole, slots, partner_bases, partner_weights, partner_rates,
    basis_h, basis_l, other_h, other_l, block_h, block_l, proj_h, proj_l,
    f0_h, f0_l, f1_h, f1_l, terms, dressed, d_send, d_recv, part_send, part_recv,
    plane_send, plane_recv, send_sem, recv_sem, local_sem,
):
    zh, y, x, zl, core = place()
    partner = device(zh, y, x, 1 - zl, core)
    twin = device(zh, y, x, zl, 1 - core)
    up, down, across = (device(zh + k, y, x, zl, core) for k in (1, 3, 2))
    step_y = 2 - zl
    fit_to = device(zh + lax.div(y + step_y, 4), y + step_y, x, zl, core)
    fit_from = device(zh + 3 + lax.div(y + 4 - step_y, 4), y + 4 - step_y, x, zl, core)

    def across_plane(t):
        return device(zh, y + lax.div(t, 4), x + lax.rem(t, 4), zl, core)

    def copy(n, src, dst, to):
        return pltpu.make_async_remote_copy(
            src_ref=src, dst_ref=dst, send_sem=send_sem.at[n], recv_sem=recv_sem.at[n],
            device_id=to, device_id_type=MESH,
        )

    def plane_copy(dz, t):
        n = dz * 16 + t
        return pltpu.make_async_remote_copy(
            src_ref=stage.at[n], dst_ref=arrived.at[n], send_sem=plane_send.at[n], recv_sem=plane_recv.at[n],
            device_id=across_plane(t), device_id_type=MESH,
        )

    sh = copy(SHARD, shard, whole.at[0, zl], partner)
    bases = copy(BASES, packed.at[:, pl.ds(0, PNO), :], partner_bases, partner)
    wts = copy(WEIGHTS, weights, partner_weights, partner)
    tabs = {dz: copy(TABLE + dz, table, tables_in.at[dz], to) for dz, to in ((1, up), (2, across), (3, down))}
    scls = {dz: copy(SCALES + dz, scales, scales_in.at[dz], to) for dz, to in ((1, up), (2, across), (3, down))}
    back = {dz: copy(PARTS + dz, z_send.at[dz], z_part.at[dz], to) for dz, to in ((1, down), (2, across), (3, up))}
    rows = pl.ds(0, PNO)

    def z_up(i):
        return copy(UP + i, packed.at[i, rows], z1.at[i], up)

    def z_down(i):
        return copy(DOWN + i, packed.at[i, rows], z3.at[i], down)

    def relay_up(i):
        return copy(RELAY + i, z1.at[i], z2.at[i], up)

    def relay_down(i):
        return copy(RELAY + i, z3.at[i], z2.at[i], down)

    def fy(a):
        return copy(FY + a, whole.at[0, a], whole.at[1, a], fit_to)


    def aside(a):
        return copy(DETOUR + a, whole.at[0, a], detour.at[a], device(zh, 1, x, zl, core))

    def onward(a):
        return pltpu.make_async_remote_copy(
            src_ref=detour.at[a], dst_ref=whole.at[1, a], send_sem=send_sem.at[ONWARD + a], recv_sem=recv_sem.at[FY + a],
            device_id=up, device_id_type=MESH,
        )

    turns = (1 - zl) * lax.div(y, 3)
    bends = (1 - zl) * lax.rem(y, 2) * (1 - lax.div(y, 3))

    def fx(dx, which, i):
        a, k = i // 2, i % 2
        return copy(
            FX + dx * 4 + i, whole.at[which, a, k], slots.at[dx, a, core, k], device(zh, y, x + dx, zl, core)
        )

    def send_rows(which, pieces):
        for i in pieces:
            for dx in (1, 3, 2):

                @pl.when(own_rows(dx) == 1 - which)
                def _():
                    fx(dx, which, i).start()

    def to_twin(j):
        return copy(CORE + j, slots.at[j, :, core], slots.at[j, :, core], twin)

    def first_slot(which):
        pltpu.make_async_copy(whole.at[which], slots.at[0, :, core], local_sem.at[1]).start()
        copy(CORE, whole.at[which], slots.at[0, :, core], twin).start()

    def fill_stage(dz):
        def picked(t):
            group = lax.rem(zh + 4 - dz, 4) * 4 + lax.rem(y + lax.div(t, 4), 4)
            return packed[sends_ref[group * 4 + lax.rem(x + lax.rem(t, 4), 4)]]

        arrived[dz * 16] = picked(0)

        def one(t, _):
            stage[dz * 16 + t] = picked(t)
            return 0

        lax.fori_loop(1, 16, one, 0)

    def send_stage(dz):
        for t in (1, 4, 3, 12, 5, 7, 13, 15, 2, 8, 6, 9, 14, 11, 10):
            plane_copy(dz, t).start()

    barrier = pltpu.get_barrier_semaphore()

    def greet(to):
        pl.semaphore_signal(barrier, inc=1, device_id=to, device_id_type=MESH)

    def greet_plane(t, _):
        greet(across_plane(t))
        return 0

    lax.fori_loop(1, 16, greet_plane, 0)
    for to in (partner, twin, up, down, across, fit_to, fit_from):
        greet(to)
    own_shard = pltpu.make_async_copy(shard, whole.at[0, zl], local_sem.at[0])
    own_shard.start()
    for dz in (1, 3, 2, 0):
        fill_stage(dz)

    def split_own(p, _):
        basis_h[0, p], basis_l[0, p] = split(packed[p, :PNO, :])
        return 0

    lax.fori_loop(0, PAIRS, split_own, 0)
    own_shard.wait()
    pl.semaphore_wait(barrier, 22)

    sh.start()
    for dz in (1, 3, 2):
        tabs[dz].start()
        scls[dz].start()
    for i in range(4):
        z_up(i).start()
        z_down(4 + i).start()
    send_stage(1)

    sh.wait_recv()

    @pl.when(turns == 1)
    def _():
        aside(0).start()
        aside(1).start()

    @pl.when(turns == 0)
    def _():
        fy(0).start()
        fy(1).start()

    def own_rows(dx):
        return (1 - zl) * (1 - lax.div(x + dx, 4))

    for i in range(4):
        z_up(4 + i).start()
        z_down(3 - i).start()
        send_rows(0, (i,))

    @pl.when(zl == 0)
    def _():
        first_slot(0)

    send_stage(3)

    @pl.when(bends == 1)
    def _():
        for a in range(2):
            aside(a).wait_recv()
            onward(a).start()

    fy(0).wait_recv()
    fy(1).wait_recv()
    for i in range(4):
        z_up(i).wait_recv()
        if i < SHIFT:
            relay_up(i).start()
        else:

            @pl.when(y == 0)
            def _():
                relay_up(i).start()

        z_down(4 + i).wait_recv()
        relay_down(4 + i).start()
        send_rows(1, (i,))

    @pl.when(zl == 1)
    def _():
        first_slot(1)

    send_stage(2)
    wts.start()
    bases.start()
    send_stage(0)
    for i in (3, 2, 1, 0):
        z_down(i).wait_recv()
        if i >= SHIFT:

            @pl.when(y > 0)
            def _():
                relay_down(i).start()

    def readers(dz, source):
        tabs[dz].wait_recv()
        scls[dz].wait_recv()
        table_in = pltpu.make_async_copy(tables_in.at[dz], tables_sm.at[dz], local_sem.at[2])
        scale_in = pltpu.make_async_copy(scales_in.at[dz], scales_sm.at[dz], local_sem.at[3])
        table_in.start()
        scale_in.start()

        def one(p, _):
            basis_h[dz, p], basis_l[dz, p] = split(source[p])
            return 0

        lax.fori_loop(0, PAIRS, one, 0)
        table_in.wait()
        scale_in.wait()

    def dress(dz):
        def one_of(t):
            return pltpu.make_async_remote_copy(
                src_ref=stage.at[t], dst_ref=arrived.at[t], send_sem=plane_send.at[t], recv_sem=plane_recv.at[t],
                device_id=twin, device_id_type=MESH,
            )

        def arrive(t, _):
            one_of(t).wait_recv()
            return 0

        lax.fori_loop(dz * 16 + 1, dz * 16 + 16, arrive, 0)

        def some(i, _):
            for u in range(4):
                t = i * 4 + u
                term = inverse_ref[t] if dz == 0 else tables_sm[dz, 8, (4 - dz) * 16 + t]
                reader, of = lax.div(term, 8), lax.rem(term, 8)
                scale = scale_ref[reader, of] if dz == 0 else scales_sm[dz, reader, of]
                own = basis_h[dz, reader], basis_l[dz, reader]
                n = dz * 16 + t
                overlap = split(dot3(own, split(arrived[n, :PNO, :]), NT))
                half = split(dot3(overlap, split(natural(arrived[n, PNO:, :])), NN))
                terms[n] = scale * dot3(half, overlap, NT)
            return 0

        lax.fori_loop(0, 4, some, 0)

    def part(dz, p):
        total = jnp.zeros((PNO, PNO), F32)
        for c in range(8):
            slot = couple_ref[p, c] if dz == 0 else tables_sm[dz, p, c]
            here = jnp.where(lax.div(slot, 16) == zh, 1.0, 0.0)
            row = lax.rem(y + 4 - lax.rem(lax.div(slot, 4), 4), 4)
            total = total + here * terms[dz * 16 + row * 4 + lax.rem(x + 4 - lax.rem(slot, 4), 4)]
        return total

    def give_back(dz):
        def one(q, _):
            z_send[dz, q] = jnp.concatenate([part(dz, q), part(dz, q + 4)], axis=1)
            return 0

        lax.fori_loop(0, 4, one, 0)
        back[dz].start()

    def fit(j, group):
        bases_h, bases_l = (basis_h.at[0], basis_l.at[0]) if group == 0 else (other_h, other_l)
        rates = rate_ref if group == 0 else partner_rates
        late = lax.div(3 - x + j, 4)
        stop = j + 4 * (zl + late - 2 * zl * late)

        def project(n, _):
            flat = (bases_h[...].reshape(PAIRS * PNO, ORB), bases_l[...].reshape(PAIRS * PNO, ORB))
            proj_h[n], proj_l[n] = split(dot3(flat, (block_h[n], block_l[n]), NN))
            return 0

        lax.fori_loop(0, 4, project, 0)

        def pair(p, _):
            rows = pl.ds(pl.multiple_of(p * PNO, PNO), PNO)
            left = proj_h[:, rows, :].reshape(4 * PNO, ORB), proj_l[:, rows, :].reshape(4 * PNO, ORB)
            both = dot3(left, (bases_h[p], bases_l[p]), NT)
            n = group * PAIRS + p
            for k in range(2):
                to = pl.ds((j * 2 + k) * PNO, PNO)
                f0_h[n, to, :], f0_l[n, to, :] = split(both[k * PNO : (k + 1) * PNO] * rates[p, stop * 2 + k])
            right = jnp.concatenate([both[2 * PNO : 3 * PNO], both[3 * PNO :]], axis=1)
            f1_h[n, :, pl.ds(j * 128, 128)], f1_l[n, :, pl.ds(j * 128, 128)] = split(right)
            return 0

        lax.fori_loop(0, PAIRS, pair, 0)

    def load_blocks(j):
        for n in range(4):
            m, k = n // 2, n % 2
            rows = [slots[j, a, b, k, m] for a in range(2) for b in range(2)]
            block_h[n], block_l[n] = split(jnp.concatenate(rows, axis=0))

    for i in range(4):
        z_up(4 + i).wait_recv()
    readers(1, z1)
    readers(3, z3)
    dress(1)
    give_back(1)
    to_twin(0).wait_recv()
    pltpu.make_async_copy(whole.at[0], slots.at[0, :, core], local_sem.at[1]).wait()
    load_blocks(0)
    fit(0, 0)
    for dx in (1, 3, 2):
        for i in range(4):
            fx(dx, 0, i).wait_recv()
        to_twin(dx).start()
    wts.wait_recv()
    rates_in = pltpu.make_async_copy(partner_weights, partner_rates, local_sem.at[1])
    rates_in.start()
    bases.wait_recv()
    rates_in.wait()

    def split_other(p, _):
        other_h[p], other_l[p] = split(partner_bases[p])
        return 0

    lax.fori_loop(0, PAIRS, split_other, 0)
    fit(0, 1)
    dress(3)
    give_back(3)
    for i in range(8):
        relay_up(i).wait_recv()
    readers(2, z2)
    for j in (1, 3):
        to_twin(j).wait_recv()
        load_blocks(j)
        fit(j, 0)
        fit(j, 1)
    dress(2)
    give_back(2)
    to_twin(2).wait_recv()
    load_blocks(2)
    fit(2, 0)
    fit(2, 1)
    dress(0)

    def gather_terms(p, _):
        dressed[p] = natural(packed[p, PNO:, :]) + part(0, p)
        return 0

    lax.fori_loop(0, PAIRS, gather_terms, 0)
    for dz in (1, 3, 2):
        back[dz].wait_recv()

    def gather_parts(q, _):
        two = z_part[1, q] + z_part[2, q] + z_part[3, q]
        dressed[q] = dressed[q] + two[:, :PNO]
        dressed[q + 4] = dressed[q + 4] + two[:, PNO:]
        return 0

    lax.fori_loop(0, 4, gather_parts, 0)
    for q in range(4):
        d_send[q] = jnp.concatenate([dressed[q], dressed[q + 4]], axis=1)
    ds = copy(DSEND, d_send, d_recv, partner)
    ds.start()

    def fitted_sum(n, d):
        left = dot3((f0_h[n], f0_l[n]), split(d), NN)
        left = jnp.concatenate(
            [jnp.concatenate([left[i * PNO : (i + 1) * PNO], left[(i + 1) * PNO : (i + 2) * PNO]], axis=1) for i in (0, 2, 4, 6)],
            axis=1,
        )
        return dot3(split(left), (f1_h[n], f1_l[n]), NT)

    def finish_own(p, _):
        dressed[p] = dressed[p] + fitted_sum(p, dressed[p])
        return 0

    lax.fori_loop(0, PAIRS, finish_own, 0)
    ds.wait_recv()

    def finish_other(q, _):
        two = d_recv[q]
        part_send[q] = jnp.concatenate(
            [fitted_sum(PAIRS + q, two[:, :PNO]), fitted_sum(PAIRS + q + 4, two[:, PNO:])], axis=1
        )
        return 0

    lax.fori_loop(0, 4, finish_other, 0)
    ps = copy(PSEND, part_send, part_recv, partner)
    ps.start()

    for done in (sh, bases, wts, ds, *tabs.values(), *scls.values(), *back.values()):
        done.wait_send()

    @pl.when(turns == 1)
    def _():
        aside(0).wait_send()
        aside(1).wait_send()

    @pl.when(turns == 0)
    def _():
        fy(0).wait_send()
        fy(1).wait_send()

    @pl.when(bends == 1)
    def _():
        onward(0).wait_send()
        onward(1).wait_send()

    for i in range(8):
        z_up(i).wait_send()
        z_down(i).wait_send()
        relay_up(i).wait_send()
    for dx in (1, 2, 3):
        for i in range(4):
            fx(dx, 0, i).wait_send()
    for j in range(4):
        to_twin(j).wait_send()

    def plane_sent(n, _):
        @pl.when(lax.rem(n, 16) > 0)
        def _():
            plane_copy(lax.div(n, 16), lax.rem(n, 16)).wait_send()

        return 0

    lax.fori_loop(0, SLOTS, plane_sent, 0)
    ps.wait()
    for q in range(4):
        two = part_recv[q]
        out_ref[q] = dressed[q] + two[:, :PNO]
        out_ref[q + 4] = dressed[q + 4] + two[:, PNO:]


def on_device(pno_basis, amplitudes, send_list, couple, couple_weight, fit_weight, fit_blocks):
    zh, y, x, zl, _ = place()
    quarters = amplitudes.reshape(PAIRS, 4, 16, PNO).transpose(0, 2, 1, 3).reshape(PAIRS, 16, ORB)
    packed = jnp.concatenate([pno_basis, quarters], axis=1)

    t = jnp.arange(SLOTS, dtype=jnp.int32)
    source = ((zh + 4 - t // 16) % 4) * 16 + ((y + 4 - (t // 4) % 4) % 4) * 4 + (x + 4 - t % 4) % 4
    term = jnp.arange(PAIRS, dtype=jnp.int32)[:, None] * 8 + jnp.arange(8, dtype=jnp.int32)[None, :]
    inverse = jnp.sum(jnp.where(couple[None] == source[:, None, None], term[None], 0), axis=(1, 2))
    sends = send_list.reshape(SLOTS)
    table = jnp.concatenate(
        [jnp.pad(couple, ((0, 0), (0, 120))), jnp.broadcast_to(jnp.pad(inverse.reshape(1, SLOTS), ((0, 0), (0, 64))), (8, 128))]
    )
    scales = jnp.pad(couple_weight, ((0, 0), (0, 120)))
    weights = jnp.pad(fit_weight, ((0, 0), (0, 112)))

    vmem, smem = pl.BlockSpec(memory_space=pltpu.VMEM), pl.BlockSpec(memory_space=pltpu.SMEM)
    tile = functools.partial(pltpu.VMEM, dtype=F32)
    narrow = functools.partial(pltpu.VMEM, dtype=BF)
    out = pl.pallas_call(
        kernel,
        out_shape=jax.ShapeDtypeStruct((PAIRS, PNO, PNO), F32),
        in_specs=[smem] * 5 + [vmem] * 5,
        out_specs=vmem,
        scratch_shapes=[
            tile((PAIRS, PNO, ORB)), tile((PAIRS, PNO, ORB)), tile((PAIRS, PNO, ORB)),
            tile((2, 2, 2, PNO, ORB)),
            pltpu.VMEM((4, 16, 128), jnp.int32), pltpu.SMEM((4, 16, 128), jnp.int32),
            tile((4, 8, 128)), pltpu.SMEM((4, 8, 128), F32), tile((4, 4, PNO, 128)), tile((4, 4, PNO, 128)),
            tile((SLOTS, ROWS, ORB)), tile((SLOTS, ROWS, ORB)),
            tile((2, 2, 2, 2, PNO, ORB)), tile((4, 2, 2, 2, 2, PNO, ORB)),
            tile((PAIRS, PNO, ORB)), tile((PAIRS, 128)), pltpu.SMEM((PAIRS, 128), F32),
            narrow((4, PAIRS, PNO, ORB)), narrow((4, PAIRS, PNO, ORB)), narrow((PAIRS, PNO, ORB)), narrow((PAIRS, PNO, ORB)),
            narrow((4, ORB, ORB)), narrow((4, ORB, ORB)),
            narrow((4, PAIRS * PNO, ORB)), narrow((4, PAIRS * PNO, ORB)),
            narrow((16, 512, PNO)), narrow((16, 512, PNO)), narrow((16, PNO, 512)), narrow((16, PNO, 512)),
            tile((SLOTS, PNO, PNO)), tile((PAIRS, PNO, PNO)),
            tile((4, PNO, 128)), tile((4, PNO, 128)), tile((4, PNO, 128)), tile((4, PNO, 128)),
            pltpu.SemaphoreType.DMA((SLOTS,)), pltpu.SemaphoreType.DMA((SLOTS,)),
            pltpu.SemaphoreType.DMA((TRANSFERS,)), pltpu.SemaphoreType.DMA((TRANSFERS,)),
            pltpu.SemaphoreType.DMA((5,)),
        ],
        compiler_params=pltpu.CompilerParams(
            collective_id=0, has_side_effects=True, vmem_limit_bytes=60 * 1024 * 1024
        ),
    )(sends, inverse, couple, couple_weight, fit_weight, packed, fit_blocks, weights, table, scales)
    return out.reshape(PAIRS, PNO * PNO)


def solution(mesh):
    placed = (
        P(("blk", "dom"), None, None),
        P(("blk", "dom"), None),
        P("blk", "dom", None, None),
        P(("blk", "dom"), None),
        P(("blk", "dom"), None),
        P(("blk", "dom"), None),
        P("blk", None, "dom", None),
    )
    return jax.shard_map(
        on_device, mesh=mesh, in_specs=placed, out_specs=P(("blk", "dom"), None), check_vma=False
    )
```

```python
import functools

import jax
import jax.numpy as jnp
from jax import lax
from jax.experimental import pallas as pl
from jax.experimental.pallas import tpu as pltpu
from jax.sharding import PartitionSpec as P

MESH = pl.DeviceIdType.MESH
BF, F32 = jnp.bfloat16, jnp.float32
PAIRS, PNO, ORB = 8, 64, 256
ROWS = PNO + 16
SLOTS = 64
SHIFT = 3

SHARD, BASES, WEIGHTS, TABLE, DSEND, PSEND, FY, CORE, UP, DOWN, RELAY, FX, DETOUR, ONWARD, SCALES, PARTS = (
    0, 1, 2, 2, 6, 7, 8, 16, 20, 28, 36, 40, 56, 58, 59, 62,
)
TRANSFERS = 66
NN = (((1,), (0,)), ((), ()))
NT = (((1,), (1,)), ((), ()))


def split(v):
    high = v.astype(BF)
    return high, (v - high.astype(F32)).astype(BF)


def dot3(a, b, dims):
    one = functools.partial(lax.dot_general, dimension_numbers=dims, preferred_element_type=F32)
    return one(a[0], b[0]) + (one(a[0], b[1]) + one(a[1], b[0]))


def natural(a4):
    return jnp.concatenate([a4[:, PNO * u : PNO * (u + 1)] for u in range(4)], axis=0)


def place():
    blk, dom = lax.axis_index("blk"), lax.axis_index("dom")
    return lax.div(blk, 16), lax.rem(lax.div(blk, 4), 4), lax.rem(blk, 4), lax.div(dom, 2), lax.rem(dom, 2)


def device(zh, y, x, zl, core):
    return (lax.rem(zh, 4) * 4 + lax.rem(y, 4)) * 4 + lax.rem(x, 4), zl * 2 + core


def kernel(
    sends_ref, inverse_ref, couple_ref, scale_ref, rate_ref,
    packed, shard, weights, table, scales,
    out_ref,
    z1, z2, z3, detour, tables_in, tables_sm, scales_in, scales_sm, z_send, z_part, stage, arrived, whole, slots, partner_bases, partner_weights, partner_rates,
    basis_h, basis_l, other_h, other_l, block_h, block_l, proj_h, proj_l,
    f0_h, f0_l, f1_h, f1_l, terms, dressed, d_send, d_recv, part_send, part_recv,
    plane_send, plane_recv, send_sem, recv_sem, local_sem,
):
    zh, y, x, zl, core = place()
    partner = device(zh, y, x, 1 - zl, core)
    twin = device(zh, y, x, zl, 1 - core)
    up, down, across = (device(zh + k, y, x, zl, core) for k in (1, 3, 2))
    step_y = 2 - zl
    fit_to = device(zh + lax.div(y + step_y, 4), y + step_y, x, zl, core)
    fit_from = device(zh + 3 + lax.div(y + 4 - step_y, 4), y + 4 - step_y, x, zl, core)

    def across_plane(t):
        return device(zh, y + lax.div(t, 4), x + lax.rem(t, 4), zl, core)

    def copy(n, src, dst, to):
        return pltpu.make_async_remote_copy(
            src_ref=src, dst_ref=dst, send_sem=send_sem.at[n], recv_sem=recv_sem.at[n],
            device_id=to, device_id_type=MESH,
        )

    def plane_copy(dz, t):
        n = dz * 16 + t
        return pltpu.make_async_remote_copy(
            src_ref=stage.at[n], dst_ref=arrived.at[n], send_sem=plane_send.at[n], recv_sem=plane_recv.at[n],
            device_id=across_plane(t), device_id_type=MESH,
        )

    sh = copy(SHARD, shard, whole.at[0, zl], partner)
    bases = copy(BASES, packed.at[:, pl.ds(0, PNO), :], partner_bases, partner)
    wts = copy(WEIGHTS, weights, partner_weights, partner)
    tabs = {dz: copy(TABLE + dz, table, tables_in.at[dz], to) for dz, to in ((1, up), (2, across), (3, down))}
    scls = {dz: copy(SCALES + dz, scales, scales_in.at[dz], to) for dz, to in ((1, up), (2, across), (3, down))}
    back = {dz: copy(PARTS + dz, z_send.at[dz], z_part.at[dz], to) for dz, to in ((1, down), (2, across), (3, up))}
    rows = pl.ds(0, PNO)

    def z_up(i):
        return copy(UP + i, packed.at[i, rows], z1.at[i], up)

    def z_down(i):
        return copy(DOWN + i, packed.at[i, rows], z3.at[i], down)

    def relay_up(i):
        return copy(RELAY + i, z1.at[i], z2.at[i], up)

    def relay_down(i):
        return copy(RELAY + i, z3.at[i], z2.at[i], down)

    def fy(a):
        return copy(FY + a, whole.at[0, a], whole.at[1, a], fit_to)


    def aside(a):
        return copy(DETOUR + a, whole.at[0, a], detour.at[a], device(zh, 1, x, zl, core))

    def onward(a):
        return pltpu.make_async_remote_copy(
            src_ref=detour.at[a], dst_ref=whole.at[1, a], send_sem=send_sem.at[ONWARD + a], recv_sem=recv_sem.at[FY + a],
            device_id=up, device_id_type=MESH,
        )

    turns = (1 - zl) * lax.div(y, 3)
    bends = (1 - zl) * lax.rem(y, 2) * (1 - lax.div(y, 3))

    def fx(dx, which, i):
        a, k = i // 2, i % 2
        return copy(
            FX + dx * 4 + i, whole.at[which, a, k], slots.at[dx, a, core, k], device(zh, y, x + dx, zl, core)
        )

    def send_rows(which, pieces):
        for i in pieces:
            for dx in (1, 3, 2):

                @pl.when(own_rows(dx) == 1 - which)
                def _():
                    fx(dx, which, i).start()

    def to_twin(j):
        return copy(CORE + j, slots.at[j, :, core], slots.at[j, :, core], twin)

    def first_slot(which):
        pltpu.make_async_copy(whole.at[which], slots.at[0, :, core], local_sem.at[1]).start()
        copy(CORE, whole.at[which], slots.at[0, :, core], twin).start()

    def fill_stage(dz):
        def picked(t):
            group = lax.rem(zh + 4 - dz, 4) * 4 + lax.rem(y + lax.div(t, 4), 4)
            return packed[sends_ref[group * 4 + lax.rem(x + lax.rem(t, 4), 4)]]

        arrived[dz * 16] = picked(0)

        def one(t, _):
            stage[dz * 16 + t] = picked(t)
            return 0

        lax.fori_loop(1, 16, one, 0)

    def send_stage(dz):
        for t in (1, 4, 3, 12, 5, 7, 13, 15, 2, 8, 6, 9, 14, 11, 10):
            plane_copy(dz, t).start()

    barrier = pltpu.get_barrier_semaphore()

    def greet(to):
        pl.semaphore_signal(barrier, inc=1, device_id=to, device_id_type=MESH)

    def greet_plane(t, _):
        greet(across_plane(t))
        return 0

    lax.fori_loop(1, 16, greet_plane, 0)
    for to in (partner, twin, up, down, across, fit_to, fit_from):
        greet(to)
    own_shard = pltpu.make_async_copy(shard, whole.at[0, zl], local_sem.at[0])
    own_shard.start()
    for dz in (1, 3, 2, 0):
        fill_stage(dz)

    def split_own(p, _):
        basis_h[0, p], basis_l[0, p] = split(packed[p, :PNO, :])
        return 0

    lax.fori_loop(0, PAIRS, split_own, 0)
    own_shard.wait()
    pl.semaphore_wait(barrier, 22)

    sh.start()
    for dz in (1, 3, 2):
        tabs[dz].start()
        scls[dz].start()
    for i in range(4):
        z_up(i).start()
        z_down(4 + i).start()
    send_stage(0)

    sh.wait_recv()

    @pl.when(turns == 1)
    def _():
        aside(0).start()
        aside(1).start()

    @pl.when(turns == 0)
    def _():
        fy(0).start()
        fy(1).start()

    def own_rows(dx):
        return (1 - zl) * (1 - lax.div(x + dx, 4))

    for i in range(4):
        z_up(4 + i).start()
        z_down(3 - i).start()
        send_rows(0, (i,))

    @pl.when(zl == 0)
    def _():
        first_slot(0)

    send_stage(1)

    @pl.when(bends == 1)
    def _():
        for a in range(2):
            aside(a).wait_recv()
            onward(a).start()

    def readers(dz, source):
        tabs[dz].wait_recv()
        scls[dz].wait_recv()
        table_in = pltpu.make_async_copy(tables_in.at[dz], tables_sm.at[dz], local_sem.at[2])
        scale_in = pltpu.make_async_copy(scales_in.at[dz], scales_sm.at[dz], local_sem.at[3])
        table_in.start()
        scale_in.start()

        def one(p, _):
            basis_h[dz, p], basis_l[dz, p] = split(source[p])
            return 0

        lax.fori_loop(0, PAIRS, one, 0)
        table_in.wait()
        scale_in.wait()

    def dress(dz):
        def one_of(t):
            return pltpu.make_async_remote_copy(
                src_ref=stage.at[t], dst_ref=arrived.at[t], send_sem=plane_send.at[t], recv_sem=plane_recv.at[t],
                device_id=twin, device_id_type=MESH,
            )

        def arrive(t, _):
            one_of(t).wait_recv()
            return 0

        lax.fori_loop(dz * 16 + 1, dz * 16 + 16, arrive, 0)

        def some(i, _):
            for u in range(4):
                t = i * 4 + u
                term = inverse_ref[t] if dz == 0 else tables_sm[dz, 8, (4 - dz) * 16 + t]
                reader, of = lax.div(term, 8), lax.rem(term, 8)
                scale = scale_ref[reader, of] if dz == 0 else scales_sm[dz, reader, of]
                own = basis_h[dz, reader], basis_l[dz, reader]
                n = dz * 16 + t
                overlap = split(dot3(own, split(arrived[n, :PNO, :]), NT))
                half = split(dot3(overlap, split(natural(arrived[n, PNO:, :])), NN))
                terms[n] = scale * dot3(half, overlap, NT)
            return 0

        lax.fori_loop(0, 4, some, 0)

    def part(dz, p):
        total = jnp.zeros((PNO, PNO), F32)
        for c in range(8):
            slot = couple_ref[p, c] if dz == 0 else tables_sm[dz, p, c]
            here = jnp.where(lax.div(slot, 16) == zh, 1.0, 0.0)
            row = lax.rem(y + 4 - lax.rem(lax.div(slot, 4), 4), 4)
            total = total + here * terms[dz * 16 + row * 4 + lax.rem(x + 4 - lax.rem(slot, 4), 4)]
        return total

    def give_back(dz):
        def one(q, _):
            z_send[dz, q] = jnp.concatenate([part(dz, q), part(dz, q + 4)], axis=1)
            return 0

        lax.fori_loop(0, 4, one, 0)
        back[dz].start()

    def fit(j, group):
        bases_h, bases_l = (basis_h.at[0], basis_l.at[0]) if group == 0 else (other_h, other_l)
        rates = rate_ref if group == 0 else partner_rates
        late = lax.div(3 - x + j, 4)
        stop = j + 4 * (zl + late - 2 * zl * late)

        def project(n, _):
            flat = (bases_h[...].reshape(PAIRS * PNO, ORB), bases_l[...].reshape(PAIRS * PNO, ORB))
            proj_h[n], proj_l[n] = split(dot3(flat, (block_h[n], block_l[n]), NN))
            return 0

        lax.fori_loop(0, 4, project, 0)

        def pair(p, _):
            rows = pl.ds(pl.multiple_of(p * PNO, PNO), PNO)
            left = proj_h[:, rows, :].reshape(4 * PNO, ORB), proj_l[:, rows, :].reshape(4 * PNO, ORB)
            both = dot3(left, (bases_h[p], bases_l[p]), NT)
            n = group * PAIRS + p
            for k in range(2):
                to = pl.ds((j * 2 + k) * PNO, PNO)
                f0_h[n, to, :], f0_l[n, to, :] = split(both[k * PNO : (k + 1) * PNO] * rates[p, stop * 2 + k])
            right = jnp.concatenate([both[2 * PNO : 3 * PNO], both[3 * PNO :]], axis=1)
            f1_h[n, :, pl.ds(j * 128, 128)], f1_l[n, :, pl.ds(j * 128, 128)] = split(right)
            return 0

        lax.fori_loop(0, PAIRS, pair, 0, unroll=4)

    def load_blocks(j):
        for n in range(4):
            m, k = n // 2, n % 2
            rows = [slots[j, a, b, k, m] for a in range(2) for b in range(2)]
            block_h[n], block_l[n] = split(jnp.concatenate(rows, axis=0))

    dress(0)
    fy(0).wait_recv()
    fy(1).wait_recv()
    for i in range(4):
        z_up(i).wait_recv()
        if i < SHIFT:
            relay_up(i).start()
        else:

            @pl.when(y == 0)
            def _():
                relay_up(i).start()

        z_down(4 + i).wait_recv()
        relay_down(4 + i).start()
        send_rows(1, (i,))

    @pl.when(zl == 1)
    def _():
        first_slot(1)

    send_stage(3)
    wts.start()
    bases.start()
    send_stage(2)
    for i in (3, 2, 1, 0):
        z_down(i).wait_recv()
        if i >= SHIFT:

            @pl.when(y > 0)
            def _():
                relay_down(i).start()

    to_twin(0).wait_recv()
    pltpu.make_async_copy(whole.at[0], slots.at[0, :, core], local_sem.at[1]).wait()
    load_blocks(0)
    fit(0, 0)
    for i in range(4):
        z_up(4 + i).wait_recv()
    readers(1, z1)
    readers(3, z3)
    for dx in (1, 3):
        for i in range(4):
            fx(dx, 0, i).wait_recv()
        to_twin(dx).start()
    dress(1)
    give_back(1)
    for dx in (2,):
        for i in range(4):
            fx(dx, 0, i).wait_recv()
        to_twin(dx).start()
    wts.wait_recv()
    rates_in = pltpu.make_async_copy(partner_weights, partner_rates, local_sem.at[1])
    rates_in.start()
    to_twin(1).wait_recv()
    rates_in.wait()
    bases.wait_recv()

    def split_other(p, _):
        other_h[p], other_l[p] = split(partner_bases[p])
        return 0

    lax.fori_loop(0, PAIRS, split_other, 0)
    fit(0, 1)
    load_blocks(1)
    fit(1, 0)
    fit(1, 1)
    dress(3)
    give_back(3)
    for i in range(8):
        relay_up(i).wait_recv()
    readers(2, z2)
    to_twin(3).wait_recv()
    load_blocks(3)
    fit(3, 0)
    fit(3, 1)
    dress(2)
    give_back(2)
    to_twin(2).wait_recv()
    load_blocks(2)
    fit(2, 0)
    fit(2, 1)

    def gather_terms(p, _):
        dressed[p] = natural(packed[p, PNO:, :]) + part(0, p)
        return 0

    lax.fori_loop(0, PAIRS, gather_terms, 0)
    for dz in (1, 3, 2):
        back[dz].wait_recv()

    def gather_parts(q, _):
        two = z_part[1, q] + z_part[2, q] + z_part[3, q]
        dressed[q] = dressed[q] + two[:, :PNO]
        dressed[q + 4] = dressed[q + 4] + two[:, PNO:]
        return 0

    lax.fori_loop(0, 4, gather_parts, 0)
    for q in range(4):
        d_send[q] = jnp.concatenate([dressed[q], dressed[q + 4]], axis=1)
    ds = copy(DSEND, d_send, d_recv, partner)
    ds.start()

    def fitted_sum(n, d):
        left = dot3((f0_h[n], f0_l[n]), split(d), NN)
        left = jnp.concatenate(
            [jnp.concatenate([left[i * PNO : (i + 1) * PNO], left[(i + 1) * PNO : (i + 2) * PNO]], axis=1) for i in (0, 2, 4, 6)],
            axis=1,
        )
        return dot3(split(left), (f1_h[n], f1_l[n]), NT)

    def finish_own(p, _):
        dressed[p] = dressed[p] + fitted_sum(p, dressed[p])
        return 0

    lax.fori_loop(0, PAIRS, finish_own, 0, unroll=4)
    ds.wait_recv()

    def finish_other(q, _):
        two = d_recv[q]
        part_send[q] = jnp.concatenate(
            [fitted_sum(PAIRS + q, two[:, :PNO]), fitted_sum(PAIRS + q + 4, two[:, PNO:])], axis=1
        )
        return 0

    lax.fori_loop(0, 4, finish_other, 0, unroll=4)
    ps = copy(PSEND, part_send, part_recv, partner)
    ps.start()

    for done in (sh, bases, wts, ds, *tabs.values(), *scls.values(), *back.values()):
        done.wait_send()

    @pl.when(turns == 1)
    def _():
        aside(0).wait_send()
        aside(1).wait_send()

    @pl.when(turns == 0)
    def _():
        fy(0).wait_send()
        fy(1).wait_send()

    @pl.when(bends == 1)
    def _():
        onward(0).wait_send()
        onward(1).wait_send()

    for i in range(8):
        z_up(i).wait_send()
        z_down(i).wait_send()
        relay_up(i).wait_send()
    for dx in (1, 2, 3):
        for i in range(4):
            fx(dx, 0, i).wait_send()
    for j in range(4):
        to_twin(j).wait_send()

    def plane_sent(n, _):
        @pl.when(lax.rem(n, 16) > 0)
        def _():
            plane_copy(lax.div(n, 16), lax.rem(n, 16)).wait_send()

        return 0

    lax.fori_loop(0, SLOTS, plane_sent, 0)
    ps.wait()
    for q in range(4):
        two = part_recv[q]
        out_ref[q] = dressed[q] + two[:, :PNO]
        out_ref[q + 4] = dressed[q + 4] + two[:, PNO:]


def on_device(pno_basis, amplitudes, send_list, couple, couple_weight, fit_weight, fit_blocks):
    zh, y, x, zl, _ = place()
    quarters = amplitudes.reshape(PAIRS, 4, 16, PNO).transpose(0, 2, 1, 3).reshape(PAIRS, 16, ORB)
    packed = jnp.concatenate([pno_basis, quarters], axis=1)

    t = jnp.arange(SLOTS, dtype=jnp.int32)
    source = ((zh + 4 - t // 16) % 4) * 16 + ((y + 4 - (t // 4) % 4) % 4) * 4 + (x + 4 - t % 4) % 4
    term = jnp.arange(PAIRS, dtype=jnp.int32)[:, None] * 8 + jnp.arange(8, dtype=jnp.int32)[None, :]
    inverse = jnp.sum(jnp.where(couple[None] == source[:, None, None], term[None], 0), axis=(1, 2))
    sends = send_list.reshape(SLOTS)
    table = jnp.concatenate(
        [jnp.pad(couple, ((0, 0), (0, 120))), jnp.broadcast_to(jnp.pad(inverse.reshape(1, SLOTS), ((0, 0), (0, 64))), (8, 128))]
    )
    scales = jnp.pad(couple_weight, ((0, 0), (0, 120)))
    weights = jnp.pad(fit_weight, ((0, 0), (0, 112)))

    vmem, smem = pl.BlockSpec(memory_space=pltpu.VMEM), pl.BlockSpec(memory_space=pltpu.SMEM)
    tile = functools.partial(pltpu.VMEM, dtype=F32)
    narrow = functools.partial(pltpu.VMEM, dtype=BF)
    out = pl.pallas_call(
        kernel,
        out_shape=jax.ShapeDtypeStruct((PAIRS, PNO, PNO), F32),
        in_specs=[smem] * 5 + [vmem] * 5,
        out_specs=vmem,
        scratch_shapes=[
            tile((PAIRS, PNO, ORB)), tile((PAIRS, PNO, ORB)), tile((PAIRS, PNO, ORB)),
            tile((2, 2, 2, PNO, ORB)),
            pltpu.VMEM((4, 16, 128), jnp.int32), pltpu.SMEM((4, 16, 128), jnp.int32),
            tile((4, 8, 128)), pltpu.SMEM((4, 8, 128), F32), tile((4, 4, PNO, 128)), tile((4, 4, PNO, 128)),
            tile((SLOTS, ROWS, ORB)), tile((SLOTS, ROWS, ORB)),
            tile((2, 2, 2, 2, PNO, ORB)), tile((4, 2, 2, 2, 2, PNO, ORB)),
            tile((PAIRS, PNO, ORB)), tile((PAIRS, 128)), pltpu.SMEM((PAIRS, 128), F32),
            narrow((4, PAIRS, PNO, ORB)), narrow((4, PAIRS, PNO, ORB)), narrow((PAIRS, PNO, ORB)), narrow((PAIRS, PNO, ORB)),
            narrow((4, ORB, ORB)), narrow((4, ORB, ORB)),
            narrow((4, PAIRS * PNO, ORB)), narrow((4, PAIRS * PNO, ORB)),
            narrow((16, 512, PNO)), narrow((16, 512, PNO)), narrow((16, PNO, 512)), narrow((16, PNO, 512)),
            tile((SLOTS, PNO, PNO)), tile((PAIRS, PNO, PNO)),
            tile((4, PNO, 128)), tile((4, PNO, 128)), tile((4, PNO, 128)), tile((4, PNO, 128)),
            pltpu.SemaphoreType.DMA((SLOTS,)), pltpu.SemaphoreType.DMA((SLOTS,)),
            pltpu.SemaphoreType.DMA((TRANSFERS,)), pltpu.SemaphoreType.DMA((TRANSFERS,)),
            pltpu.SemaphoreType.DMA((5,)),
        ],
        compiler_params=pltpu.CompilerParams(
            collective_id=0, has_side_effects=True, vmem_limit_bytes=60 * 1024 * 1024
        ),
    )(sends, inverse, couple, couple_weight, fit_weight, packed, fit_blocks, weights, table, scales)
    return out.reshape(PAIRS, PNO * PNO)


def solution(mesh):
    placed = (
        P(("blk", "dom"), None, None),
        P(("blk", "dom"), None),
        P("blk", "dom", None, None),
        P(("blk", "dom"), None),
        P(("blk", "dom"), None),
        P(("blk", "dom"), None),
        P("blk", None, "dom", None),
    )
    return jax.shard_map(
        on_device, mesh=mesh, in_specs=placed, out_specs=P(("blk", "dom"), None), check_vma=False
    )
```

```python
import functools

import jax
import jax.numpy as jnp
from jax import lax
from jax.experimental import pallas as pl
from jax.experimental.pallas import tpu as pltpu
from jax.sharding import PartitionSpec as P

MESH = pl.DeviceIdType.MESH
BF, F32 = jnp.bfloat16, jnp.float32
PAIRS, PNO, ORB = 8, 64, 256
ROWS = PNO + 16
SLOTS = 64
SHIFT = 3

SHARD, BASES, WEIGHTS, TABLE, FY, CORE, UP, DOWN, RELAY, FX, DETOUR, ONWARD, SCALES, PARTS = (
    0, 1, 2, 2, 8, 16, 20, 28, 36, 40, 56, 58, 59, 62,
)
DSEND, PSEND = (6, 7, 66, 67), (68, 69, 70, 71)
TRANSFERS = 72
NN = (((1,), (0,)), ((), ()))
NT = (((1,), (1,)), ((), ()))


def split(v):
    high = v.astype(BF)
    return high, (v - high.astype(F32)).astype(BF)


def dot3(a, b, dims):
    one = functools.partial(lax.dot_general, dimension_numbers=dims, preferred_element_type=F32)
    return one(a[0], b[0]) + (one(a[0], b[1]) + one(a[1], b[0]))


def natural(a4):
    return jnp.concatenate([a4[:, PNO * u : PNO * (u + 1)] for u in range(4)], axis=0)


def place():
    blk, dom = lax.axis_index("blk"), lax.axis_index("dom")
    return lax.div(blk, 16), lax.rem(lax.div(blk, 4), 4), lax.rem(blk, 4), lax.div(dom, 2), lax.rem(dom, 2)


def device(zh, y, x, zl, core):
    return (lax.rem(zh, 4) * 4 + lax.rem(y, 4)) * 4 + lax.rem(x, 4), zl * 2 + core


def kernel(
    sends_ref, inverse_ref, couple_ref, scale_ref, rate_ref,
    packed, shard, weights, table, scales,
    out_ref,
    z1, z2, z3, detour, tables_in, tables_sm, scales_in, scales_sm, z_send, z_part, stage, arrived, whole, slots, partner_bases, partner_weights, partner_rates,
    basis_h, basis_l, other_h, other_l, block_h, block_l, proj_h, proj_l,
    f0_h, f0_l, f1_h, f1_l, terms, dressed, d_send, d_recv, part_send, part_recv,
    plane_send, plane_recv, send_sem, recv_sem, local_sem,
):
    zh, y, x, zl, core = place()
    partner = device(zh, y, x, 1 - zl, core)
    twin = device(zh, y, x, zl, 1 - core)
    up, down, across = (device(zh + k, y, x, zl, core) for k in (1, 3, 2))
    step_y = 2 - zl
    fit_to = device(zh + lax.div(y + step_y, 4), y + step_y, x, zl, core)
    fit_from = device(zh + 3 + lax.div(y + 4 - step_y, 4), y + 4 - step_y, x, zl, core)

    def across_plane(t):
        return device(zh, y + lax.div(t, 4), x + lax.rem(t, 4), zl, core)

    def copy(n, src, dst, to):
        return pltpu.make_async_remote_copy(
            src_ref=src, dst_ref=dst, send_sem=send_sem.at[n], recv_sem=recv_sem.at[n],
            device_id=to, device_id_type=MESH,
        )

    def plane_copy(dz, t):
        n = dz * 16 + t
        return pltpu.make_async_remote_copy(
            src_ref=stage.at[n], dst_ref=arrived.at[n], send_sem=plane_send.at[n], recv_sem=plane_recv.at[n],
            device_id=across_plane(t), device_id_type=MESH,
        )

    sh = copy(SHARD, shard, whole.at[0, zl], partner)
    bases = copy(BASES, packed.at[:, pl.ds(0, PNO), :], partner_bases, partner)
    wts = copy(WEIGHTS, weights, partner_weights, partner)
    tabs = {dz: copy(TABLE + dz, table, tables_in.at[dz], to) for dz, to in ((1, up), (2, across), (3, down))}
    scls = {dz: copy(SCALES + dz, scales, scales_in.at[dz], to) for dz, to in ((1, up), (2, across), (3, down))}
    back = {dz: copy(PARTS + dz, z_send.at[dz], z_part.at[dz], to) for dz, to in ((1, down), (2, across), (3, up))}
    rows = pl.ds(0, PNO)

    def z_up(i):
        return copy(UP + i, packed.at[i, rows], z1.at[i], up)

    def z_down(i):
        return copy(DOWN + i, packed.at[i, rows], z3.at[i], down)

    def relay_up(i):
        return copy(RELAY + i, z1.at[i], z2.at[i], up)

    def relay_down(i):
        return copy(RELAY + i, z3.at[i], z2.at[i], down)

    def fy(a):
        return copy(FY + a, whole.at[0, a], whole.at[1, a], fit_to)


    def aside(a):
        return copy(DETOUR + a, whole.at[0, a], detour.at[a], device(zh, 1, x, zl, core))

    def onward(a):
        return pltpu.make_async_remote_copy(
            src_ref=detour.at[a], dst_ref=whole.at[1, a], send_sem=send_sem.at[ONWARD + a], recv_sem=recv_sem.at[FY + a],
            device_id=up, device_id_type=MESH,
        )

    turns = (1 - zl) * lax.div(y, 3)
    bends = (1 - zl) * lax.rem(y, 2) * (1 - lax.div(y, 3))

    def fx(dx, which, i):
        a, k = i // 2, i % 2
        return copy(
            FX + dx * 4 + i, whole.at[which, a, k], slots.at[dx, a, core, k], device(zh, y, x + dx, zl, core)
        )

    def send_rows(which, pieces):
        for i in pieces:
            for dx in (1, 3, 2):

                @pl.when(own_rows(dx) == 1 - which)
                def _():
                    fx(dx, which, i).start()

    def to_twin(j):
        return copy(CORE + j, slots.at[j, :, core], slots.at[j, :, core], twin)

    def first_slot(which):
        pltpu.make_async_copy(whole.at[which], slots.at[0, :, core], local_sem.at[1]).start()
        copy(CORE, whole.at[which], slots.at[0, :, core], twin).start()

    def fill_stage(dz):
        def picked(t):
            group = lax.rem(zh + 4 - dz, 4) * 4 + lax.rem(y + lax.div(t, 4), 4)
            return packed[sends_ref[group * 4 + lax.rem(x + lax.rem(t, 4), 4)]]

        arrived[dz * 16] = picked(0)

        def one(t, _):
            stage[dz * 16 + t] = picked(t)
            return 0

        lax.fori_loop(1, 16, one, 0)

    def send_stage(dz):
        for t in (1, 4, 3, 12, 5, 7, 13, 15, 2, 8, 6, 9, 14, 11, 10):
            plane_copy(dz, t).start()

    barrier = pltpu.get_barrier_semaphore()

    def greet(to):
        pl.semaphore_signal(barrier, inc=1, device_id=to, device_id_type=MESH)

    def greet_plane(t, _):
        greet(across_plane(t))
        return 0

    lax.fori_loop(1, 16, greet_plane, 0)
    for to in (partner, twin, up, down, across, fit_to, fit_from):
        greet(to)
    own_shard = pltpu.make_async_copy(shard, whole.at[0, zl], local_sem.at[0])
    own_shard.start()
    for dz in (1, 3, 2, 0):
        fill_stage(dz)

    def split_own(p, _):
        basis_h[0, p], basis_l[0, p] = split(packed[p, :PNO, :])
        return 0

    lax.fori_loop(0, PAIRS, split_own, 0)
    own_shard.wait()
    pl.semaphore_wait(barrier, 22)

    sh.start()
    for dz in (1, 3, 2):
        tabs[dz].start()
        scls[dz].start()
    for i in range(4):
        z_up(i).start()
        z_down(4 + i).start()
    send_stage(0)

    sh.wait_recv()

    @pl.when(turns == 1)
    def _():
        aside(0).start()
        aside(1).start()

    @pl.when(turns == 0)
    def _():
        fy(0).start()
        fy(1).start()

    def own_rows(dx):
        return (1 - zl) * (1 - lax.div(x + dx, 4))

    for i in range(4):
        z_up(4 + i).start()
        z_down(3 - i).start()
        send_rows(0, (i,))

    @pl.when(zl == 0)
    def _():
        first_slot(0)

    send_stage(1)

    @pl.when(bends == 1)
    def _():
        for a in range(2):
            aside(a).wait_recv()
            onward(a).start()

    def readers(dz, source):
        tabs[dz].wait_recv()
        scls[dz].wait_recv()
        table_in = pltpu.make_async_copy(tables_in.at[dz], tables_sm.at[dz], local_sem.at[2])
        scale_in = pltpu.make_async_copy(scales_in.at[dz], scales_sm.at[dz], local_sem.at[3])
        table_in.start()
        scale_in.start()

        def one(p, _):
            basis_h[dz, p], basis_l[dz, p] = split(source[p])
            return 0

        lax.fori_loop(0, PAIRS, one, 0)
        table_in.wait()
        scale_in.wait()

    def dress(dz):
        def one_of(t):
            return pltpu.make_async_remote_copy(
                src_ref=stage.at[t], dst_ref=arrived.at[t], send_sem=plane_send.at[t], recv_sem=plane_recv.at[t],
                device_id=twin, device_id_type=MESH,
            )

        def arrive(t, _):
            one_of(t).wait_recv()
            return 0

        lax.fori_loop(dz * 16 + 1, dz * 16 + 16, arrive, 0)

        def some(i, _):
            for u in range(8):
                t = i * 8 + u
                term = inverse_ref[t] if dz == 0 else tables_sm[dz, 8, (4 - dz) * 16 + t]
                reader, of = lax.div(term, 8), lax.rem(term, 8)
                scale = scale_ref[reader, of] if dz == 0 else scales_sm[dz, reader, of]
                own = basis_h[dz, reader], basis_l[dz, reader]
                n = dz * 16 + t
                overlap = split(dot3(own, split(arrived[n, :PNO, :]), NT))
                half = split(dot3(overlap, split(natural(arrived[n, PNO:, :])), NN))
                terms[n] = scale * dot3(half, overlap, NT)
            return 0

        lax.fori_loop(0, 2, some, 0)

    def part(dz, p):
        total = jnp.zeros((PNO, PNO), F32)
        for c in range(8):
            slot = couple_ref[p, c] if dz == 0 else tables_sm[dz, p, c]
            here = jnp.where(lax.div(slot, 16) == zh, 1.0, 0.0)
            row = lax.rem(y + 4 - lax.rem(lax.div(slot, 4), 4), 4)
            total = total + here * terms[dz * 16 + row * 4 + lax.rem(x + 4 - lax.rem(slot, 4), 4)]
        return total

    def give_back(dz):
        def one(q, _):
            z_send[dz, q] = jnp.concatenate([part(dz, q), part(dz, q + 4)], axis=1)
            return 0

        lax.fori_loop(0, 4, one, 0)
        back[dz].start()

    def fit(j, group):
        bases_h, bases_l = (basis_h.at[0], basis_l.at[0]) if group == 0 else (other_h, other_l)
        rates = rate_ref if group == 0 else partner_rates
        late = lax.div(3 - x + j, 4)
        stop = j + 4 * (zl + late - 2 * zl * late)

        def project(n, _):
            flat = (bases_h[...].reshape(PAIRS * PNO, ORB), bases_l[...].reshape(PAIRS * PNO, ORB))
            proj_h[n], proj_l[n] = split(dot3(flat, (block_h[n], block_l[n]), NN))
            return 0

        lax.fori_loop(0, 4, project, 0)

        def pair(p, _):
            rows = pl.ds(pl.multiple_of(p * PNO, PNO), PNO)
            left = proj_h[:, rows, :].reshape(4 * PNO, ORB), proj_l[:, rows, :].reshape(4 * PNO, ORB)
            both = dot3(left, (bases_h[p], bases_l[p]), NT)
            n = group * PAIRS + p
            for k in range(2):
                to = pl.ds((j * 2 + k) * PNO, PNO)
                f0_h[n, to, :], f0_l[n, to, :] = split(both[k * PNO : (k + 1) * PNO] * rates[p, stop * 2 + k])
            right = jnp.concatenate([both[2 * PNO : 3 * PNO], both[3 * PNO :]], axis=1)
            f1_h[n, :, pl.ds(j * 128, 128)], f1_l[n, :, pl.ds(j * 128, 128)] = split(right)
            return 0

        lax.fori_loop(0, PAIRS, pair, 0, unroll=4)

    def load_blocks(j):
        for n in range(4):
            m, k = n // 2, n % 2
            rows = [slots[j, a, b, k, m] for a in range(2) for b in range(2)]
            block_h[n], block_l[n] = split(jnp.concatenate(rows, axis=0))

    dress(0)
    fy(0).wait_recv()
    fy(1).wait_recv()
    for i in range(4):
        z_up(i).wait_recv()
        if i < SHIFT:
            relay_up(i).start()
        else:

            @pl.when(y == 0)
            def _():
                relay_up(i).start()

        z_down(4 + i).wait_recv()
        relay_down(4 + i).start()
        send_rows(1, (i,))

    @pl.when(zl == 1)
    def _():
        first_slot(1)

    send_stage(3)
    wts.start()
    bases.start()
    send_stage(2)
    for i in (3, 2, 1, 0):
        z_down(i).wait_recv()
        if i >= SHIFT:

            @pl.when(y > 0)
            def _():
                relay_down(i).start()

    to_twin(0).wait_recv()
    pltpu.make_async_copy(whole.at[0], slots.at[0, :, core], local_sem.at[1]).wait()
    load_blocks(0)
    fit(0, 0)
    for i in range(4):
        z_up(4 + i).wait_recv()
    readers(1, z1)
    readers(3, z3)
    for dx in (1, 3):
        for i in range(4):
            fx(dx, 0, i).wait_recv()
        to_twin(dx).start()
    dress(1)
    give_back(1)
    for dx in (2,):
        for i in range(4):
            fx(dx, 0, i).wait_recv()
        to_twin(dx).start()
    wts.wait_recv()
    rates_in = pltpu.make_async_copy(partner_weights, partner_rates, local_sem.at[1])
    rates_in.start()
    to_twin(1).wait_recv()
    rates_in.wait()
    bases.wait_recv()

    def split_other(p, _):
        other_h[p], other_l[p] = split(partner_bases[p])
        return 0

    lax.fori_loop(0, PAIRS, split_other, 0)
    fit(0, 1)
    load_blocks(1)
    fit(1, 0)
    fit(1, 1)
    dress(3)
    give_back(3)
    for i in range(8):
        relay_up(i).wait_recv()
    readers(2, z2)
    to_twin(3).wait_recv()
    load_blocks(3)
    fit(3, 0)
    fit(3, 1)
    dress(2)
    give_back(2)
    to_twin(2).wait_recv()
    load_blocks(2)
    fit(2, 0)
    fit(2, 1)

    def gather_terms(p, _):
        dressed[p] = natural(packed[p, PNO:, :]) + part(0, p)
        return 0

    lax.fori_loop(0, PAIRS, gather_terms, 0)
    for dz in (1, 3, 2):
        back[dz].wait_recv()

    def gather_parts(q, _):
        two = z_part[1, q] + z_part[2, q] + z_part[3, q]
        dressed[q] = dressed[q] + two[:, :PNO]
        dressed[q + 4] = dressed[q + 4] + two[:, PNO:]
        return 0

    lax.fori_loop(0, 4, gather_parts, 0)
    for q in range(4):
        d_send[q] = jnp.concatenate([dressed[q], dressed[q + 4]], axis=1)
    ds = [copy(DSEND[q], d_send.at[q], d_recv.at[q], partner) for q in range(4)]
    ps = [copy(PSEND[q], part_send.at[q], part_recv.at[q], partner) for q in range(4)]
    for q in range(4):
        ds[q].start()

    def fitted_sum(n, d):
        left = dot3((f0_h[n], f0_l[n]), split(d), NN)
        left = jnp.concatenate(
            [jnp.concatenate([left[i * PNO : (i + 1) * PNO], left[(i + 1) * PNO : (i + 2) * PNO]], axis=1) for i in (0, 2, 4, 6)],
            axis=1,
        )
        return dot3(split(left), (f1_h[n], f1_l[n]), NT)

    def finish_own(p, _):
        dressed[p] = dressed[p] + fitted_sum(p, dressed[p])
        return 0

    lax.fori_loop(0, PAIRS, finish_own, 0, unroll=4)
    for q in range(4):
        ds[q].wait_recv()
        two = d_recv[q]
        part_send[q] = jnp.concatenate(
            [fitted_sum(PAIRS + q, two[:, :PNO]), fitted_sum(PAIRS + q + 4, two[:, PNO:])], axis=1
        )
        ps[q].start()

    for done in (sh, bases, wts, *ds, *tabs.values(), *scls.values(), *back.values()):
        done.wait_send()

    @pl.when(turns == 1)
    def _():
        aside(0).wait_send()
        aside(1).wait_send()

    @pl.when(turns == 0)
    def _():
        fy(0).wait_send()
        fy(1).wait_send()

    @pl.when(bends == 1)
    def _():
        onward(0).wait_send()
        onward(1).wait_send()

    for i in range(8):
        z_up(i).wait_send()
        z_down(i).wait_send()
        relay_up(i).wait_send()
    for dx in (1, 2, 3):
        for i in range(4):
            fx(dx, 0, i).wait_send()
    for j in range(4):
        to_twin(j).wait_send()

    def plane_sent(n, _):
        @pl.when(lax.rem(n, 16) > 0)
        def _():
            plane_copy(lax.div(n, 16), lax.rem(n, 16)).wait_send()

        return 0

    lax.fori_loop(0, SLOTS, plane_sent, 0)
    for q in range(4):
        ps[q].wait()
        two = part_recv[q]
        out_ref[q] = dressed[q] + two[:, :PNO]
        out_ref[q + 4] = dressed[q + 4] + two[:, PNO:]


def on_device(pno_basis, amplitudes, send_list, couple, couple_weight, fit_weight, fit_blocks):
    zh, y, x, zl, _ = place()
    quarters = amplitudes.reshape(PAIRS, 4, 16, PNO).transpose(0, 2, 1, 3).reshape(PAIRS, 16, ORB)
    packed = jnp.concatenate([pno_basis, quarters], axis=1)

    t = jnp.arange(SLOTS, dtype=jnp.int32)
    source = ((zh + 4 - t // 16) % 4) * 16 + ((y + 4 - (t // 4) % 4) % 4) * 4 + (x + 4 - t % 4) % 4
    term = jnp.arange(PAIRS, dtype=jnp.int32)[:, None] * 8 + jnp.arange(8, dtype=jnp.int32)[None, :]
    inverse = jnp.sum(jnp.where(couple[None] == source[:, None, None], term[None], 0), axis=(1, 2))
    sends = send_list.reshape(SLOTS)
    table = jnp.concatenate(
        [jnp.pad(couple, ((0, 0), (0, 120))), jnp.broadcast_to(jnp.pad(inverse.reshape(1, SLOTS), ((0, 0), (0, 64))), (8, 128))]
    )
    scales = jnp.pad(couple_weight, ((0, 0), (0, 120)))
    weights = jnp.pad(fit_weight, ((0, 0), (0, 112)))

    vmem, smem = pl.BlockSpec(memory_space=pltpu.VMEM), pl.BlockSpec(memory_space=pltpu.SMEM)
    tile = functools.partial(pltpu.VMEM, dtype=F32)
    narrow = functools.partial(pltpu.VMEM, dtype=BF)
    out = pl.pallas_call(
        kernel,
        out_shape=jax.ShapeDtypeStruct((PAIRS, PNO, PNO), F32),
        in_specs=[smem] * 5 + [vmem] * 5,
        out_specs=vmem,
        scratch_shapes=[
            tile((PAIRS, PNO, ORB)), tile((PAIRS, PNO, ORB)), tile((PAIRS, PNO, ORB)),
            tile((2, 2, 2, PNO, ORB)),
            pltpu.VMEM((4, 16, 128), jnp.int32), pltpu.SMEM((4, 16, 128), jnp.int32),
            tile((4, 8, 128)), pltpu.SMEM((4, 8, 128), F32), tile((4, 4, PNO, 128)), tile((4, 4, PNO, 128)),
            tile((SLOTS, ROWS, ORB)), tile((SLOTS, ROWS, ORB)),
            tile((2, 2, 2, 2, PNO, ORB)), tile((4, 2, 2, 2, 2, PNO, ORB)),
            tile((PAIRS, PNO, ORB)), tile((PAIRS, 128)), pltpu.SMEM((PAIRS, 128), F32),
            narrow((4, PAIRS, PNO, ORB)), narrow((4, PAIRS, PNO, ORB)), narrow((PAIRS, PNO, ORB)), narrow((PAIRS, PNO, ORB)),
            narrow((4, ORB, ORB)), narrow((4, ORB, ORB)),
            narrow((4, PAIRS * PNO, ORB)), narrow((4, PAIRS * PNO, ORB)),
            narrow((16, 512, PNO)), narrow((16, 512, PNO)), narrow((16, PNO, 512)), narrow((16, PNO, 512)),
            tile((SLOTS, PNO, PNO)), tile((PAIRS, PNO, PNO)),
            tile((4, PNO, 128)), tile((4, PNO, 128)), tile((4, PNO, 128)), tile((4, PNO, 128)),
            pltpu.SemaphoreType.DMA((SLOTS,)), pltpu.SemaphoreType.DMA((SLOTS,)),
            pltpu.SemaphoreType.DMA((TRANSFERS,)), pltpu.SemaphoreType.DMA((TRANSFERS,)),
            pltpu.SemaphoreType.DMA((5,)),
        ],
        compiler_params=pltpu.CompilerParams(
            collective_id=0, has_side_effects=True, vmem_limit_bytes=60 * 1024 * 1024
        ),
    )(sends, inverse, couple, couple_weight, fit_weight, packed, fit_blocks, weights, table, scales)
    return out.reshape(PAIRS, PNO * PNO)


def solution(mesh):
    placed = (
        P(("blk", "dom"), None, None),
        P(("blk", "dom"), None),
        P("blk", "dom", None, None),
        P(("blk", "dom"), None),
        P(("blk", "dom"), None),
        P(("blk", "dom"), None),
        P("blk", None, "dom", None),
    )
    return jax.shard_map(
        on_device, mesh=mesh, in_specs=placed, out_specs=P(("blk", "dom"), None), check_vma=False
    )
```

```python
import functools

import jax
import jax.numpy as jnp
from jax import lax
from jax.experimental import pallas as pl
from jax.experimental.pallas import tpu as pltpu
from jax.sharding import PartitionSpec as P

MESH = pl.DeviceIdType.MESH
BF, F32 = jnp.bfloat16, jnp.float32
PAIRS, PNO, ORB = 8, 64, 256
ROWS = PNO + 16
SLOTS = 64
SHIFT = 3

SHARD, BASES, WEIGHTS, TABLE, FY, CORE, UP, DOWN, RELAY, FX, DETOUR, ONWARD, SCALES, PARTS = (
    0, 1, 2, 2, 8, 16, 20, 28, 36, 40, 56, 58, 59, 62,
)
DSEND, PSEND = (6, 7, 66, 67), (68, 69, 70, 71)
TRANSFERS = 72
NN = (((1,), (0,)), ((), ()))
NT = (((1,), (1,)), ((), ()))


def split(v):
    high = v.astype(BF)
    return high, (v - high.astype(F32)).astype(BF)


def dot3(a, b, dims):
    one = functools.partial(lax.dot_general, dimension_numbers=dims, preferred_element_type=F32)
    return one(a[0], b[0]) + (one(a[0], b[1]) + one(a[1], b[0]))


def natural(a4):
    return jnp.concatenate([a4[:, PNO * u : PNO * (u + 1)] for u in range(4)], axis=0)


def place():
    blk, dom = lax.axis_index("blk"), lax.axis_index("dom")
    return lax.div(blk, 16), lax.rem(lax.div(blk, 4), 4), lax.rem(blk, 4), lax.div(dom, 2), lax.rem(dom, 2)


def device(zh, y, x, zl, core):
    return (lax.rem(zh, 4) * 4 + lax.rem(y, 4)) * 4 + lax.rem(x, 4), zl * 2 + core


def kernel(
    sends_ref, inverse_ref, couple_ref, scale_ref, rate_ref,
    packed, shard, weights, table, scales,
    out_ref,
    z1, z2, z3, detour, tables_in, tables_sm, scales_in, scales_sm, z_send, z_part, stage, arrived, whole, slots, partner_bases, partner_weights, partner_rates,
    basis_h, basis_l, other_h, other_l, block_h, block_l, proj_h, proj_l,
    f0_h, f0_l, f1_h, f1_l, terms, dressed, d_send, d_recv, part_send, part_recv,
    plane_send, plane_recv, send_sem, recv_sem, local_sem,
):
    zh, y, x, zl, core = place()
    partner = device(zh, y, x, 1 - zl, core)
    twin = device(zh, y, x, zl, 1 - core)
    up, down, across = (device(zh + k, y, x, zl, core) for k in (1, 3, 2))
    step_y = 2 - zl
    fit_to = device(zh + lax.div(y + step_y, 4), y + step_y, x, zl, core)
    fit_from = device(zh + 3 + lax.div(y + 4 - step_y, 4), y + 4 - step_y, x, zl, core)

    def across_plane(t):
        return device(zh, y + lax.div(t, 4), x + lax.rem(t, 4), zl, core)

    def copy(n, src, dst, to):
        return pltpu.make_async_remote_copy(
            src_ref=src, dst_ref=dst, send_sem=send_sem.at[n], recv_sem=recv_sem.at[n],
            device_id=to, device_id_type=MESH,
        )

    def plane_copy(dz, t):
        n = dz * 16 + t
        return pltpu.make_async_remote_copy(
            src_ref=stage.at[n], dst_ref=arrived.at[n], send_sem=plane_send.at[n], recv_sem=plane_recv.at[n],
            device_id=across_plane(t), device_id_type=MESH,
        )

    sh = copy(SHARD, shard, whole.at[0, zl], partner)
    bases = copy(BASES, packed.at[:, pl.ds(0, PNO), :], partner_bases, partner)
    wts = copy(WEIGHTS, weights, partner_weights, partner)
    tabs = {dz: copy(TABLE + dz, table, tables_in.at[dz], to) for dz, to in ((1, up), (2, across), (3, down))}
    scls = {dz: copy(SCALES + dz, scales, scales_in.at[dz], to) for dz, to in ((1, up), (2, across), (3, down))}
    back = {dz: copy(PARTS + dz, z_send.at[dz], z_part.at[dz], to) for dz, to in ((1, down), (2, across), (3, up))}
    rows = pl.ds(0, PNO)

    def z_up(i):
        return copy(UP + i, packed.at[i, rows], z1.at[i], up)

    def z_down(i):
        return copy(DOWN + i, packed.at[i, rows], z3.at[i], down)

    def relay_up(i):
        return copy(RELAY + i, z1.at[i], z2.at[i], up)

    def relay_down(i):
        return copy(RELAY + i, z3.at[i], z2.at[i], down)

    def fy(a):
        return copy(FY + a, whole.at[0, a], whole.at[1, a], fit_to)


    def aside(a):
        return copy(DETOUR + a, whole.at[0, a], detour.at[a], device(zh, 1, x, zl, core))

    def onward(a):
        return pltpu.make_async_remote_copy(
            src_ref=detour.at[a], dst_ref=whole.at[1, a], send_sem=send_sem.at[ONWARD + a], recv_sem=recv_sem.at[FY + a],
            device_id=up, device_id_type=MESH,
        )

    turns = (1 - zl) * lax.div(y, 3)
    bends = (1 - zl) * lax.rem(y, 2) * (1 - lax.div(y, 3))

    def fx(dx, which, i):
        a, k = i // 2, i % 2
        return copy(
            FX + dx * 4 + i, whole.at[which, a, k], slots.at[dx, a, core, k], device(zh, y, x + dx, zl, core)
        )

    def send_rows(which, pieces):
        for i in pieces:
            for dx in (1, 3, 2):

                @pl.when(own_rows(dx) == 1 - which)
                def _():
                    fx(dx, which, i).start()

    def to_twin(j):
        return copy(CORE + j, slots.at[j, :, core], slots.at[j, :, core], twin)

    def first_slot(which):
        pltpu.make_async_copy(whole.at[which], slots.at[0, :, core], local_sem.at[1]).start()
        copy(CORE, whole.at[which], slots.at[0, :, core], twin).start()

    def fill_stage(dz):
        def picked(t):
            group = lax.rem(zh + 4 - dz, 4) * 4 + lax.rem(y + lax.div(t, 4), 4)
            return packed[sends_ref[group * 4 + lax.rem(x + lax.rem(t, 4), 4)]]

        arrived[dz * 16] = picked(0)

        def one(t, _):
            stage[dz * 16 + t] = picked(t)
            return 0

        lax.fori_loop(1, 16, one, 0)

    def send_stage(dz):
        for t in (1, 4, 3, 12, 5, 7, 13, 15, 2, 8, 6, 9, 14, 11, 10):
            plane_copy(dz, t).start()

    barrier = pltpu.get_barrier_semaphore()

    def greet(to):
        pl.semaphore_signal(barrier, inc=1, device_id=to, device_id_type=MESH)

    def greet_plane(t, _):
        greet(across_plane(t))
        return 0

    lax.fori_loop(1, 16, greet_plane, 0)
    for to in (partner, twin, up, down, across, fit_to, fit_from):
        greet(to)
    own_shard = pltpu.make_async_copy(shard, whole.at[0, zl], local_sem.at[0])
    own_shard.start()
    for dz in (1, 3, 2, 0):
        fill_stage(dz)

    def split_own(p, _):
        basis_h[0, p], basis_l[0, p] = split(packed[p, :PNO, :])
        return 0

    lax.fori_loop(0, PAIRS, split_own, 0)
    own_shard.wait()
    pl.semaphore_wait(barrier, 22)

    sh.start()
    for dz in (1, 3, 2):
        tabs[dz].start()
        scls[dz].start()
    for i in range(4):
        z_up(i).start()
        z_down(4 + i).start()
    send_stage(0)

    sh.wait_recv()

    @pl.when(turns == 1)
    def _():
        aside(0).start()
        aside(1).start()

    @pl.when(turns == 0)
    def _():
        fy(0).start()
        fy(1).start()

    def own_rows(dx):
        return (1 - zl) * (1 - lax.div(x + dx, 4))

    for i in range(4):
        z_up(4 + i).start()
        z_down(3 - i).start()
        send_rows(0, (i,))

    @pl.when(zl == 0)
    def _():
        first_slot(0)

    send_stage(1)

    @pl.when(bends == 1)
    def _():
        for a in range(2):
            aside(a).wait_recv()
            onward(a).start()

    def readers(dz, source):
        tabs[dz].wait_recv()
        scls[dz].wait_recv()
        table_in = pltpu.make_async_copy(tables_in.at[dz], tables_sm.at[dz], local_sem.at[2])
        scale_in = pltpu.make_async_copy(scales_in.at[dz], scales_sm.at[dz], local_sem.at[3])
        table_in.start()
        scale_in.start()

        def one(p, _):
            basis_h[dz, p], basis_l[dz, p] = split(source[p])
            return 0

        lax.fori_loop(0, PAIRS, one, 0)
        table_in.wait()
        scale_in.wait()

    def dress(dz):
        def one_of(t):
            return pltpu.make_async_remote_copy(
                src_ref=stage.at[t], dst_ref=arrived.at[t], send_sem=plane_send.at[t], recv_sem=plane_recv.at[t],
                device_id=twin, device_id_type=MESH,
            )

        def arrive(t, _):
            one_of(t).wait_recv()
            return 0

        lax.fori_loop(dz * 16 + 1, dz * 16 + 16, arrive, 0)

        def some(i, _):
            for u in range(8):
                t = i * 8 + u
                term = inverse_ref[t] if dz == 0 else tables_sm[dz, 8, (4 - dz) * 16 + t]
                reader, of = lax.div(term, 8), lax.rem(term, 8)
                scale = scale_ref[reader, of] if dz == 0 else scales_sm[dz, reader, of]
                own = basis_h[dz, reader], basis_l[dz, reader]
                n = dz * 16 + t
                overlap = split(dot3(own, split(arrived[n, :PNO, :]), NT))
                half = split(dot3(overlap, split(natural(arrived[n, PNO:, :])), NN))
                terms[n] = scale * dot3(half, overlap, NT)
            return 0

        lax.fori_loop(0, 2, some, 0)

    def part(dz, p):
        total = jnp.zeros((PNO, PNO), F32)
        for c in range(8):
            slot = couple_ref[p, c] if dz == 0 else tables_sm[dz, p, c]
            here = jnp.where(lax.div(slot, 16) == zh, 1.0, 0.0)
            row = lax.rem(y + 4 - lax.rem(lax.div(slot, 4), 4), 4)
            total = total + here * terms[dz * 16 + row * 4 + lax.rem(x + 4 - lax.rem(slot, 4), 4)]
        return total

    def give_back(dz):
        def one(q, _):
            z_send[dz, q] = jnp.concatenate([part(dz, q), part(dz, q + 4)], axis=1)
            return 0

        lax.fori_loop(0, 4, one, 0, unroll=2)
        back[dz].start()

    def fit(j, group):
        bases_h, bases_l = (basis_h.at[0], basis_l.at[0]) if group == 0 else (other_h, other_l)
        rates = rate_ref if group == 0 else partner_rates
        late = lax.div(3 - x + j, 4)
        stop = j + 4 * (zl + late - 2 * zl * late)

        def project(n, _):
            flat = (bases_h[...].reshape(PAIRS * PNO, ORB), bases_l[...].reshape(PAIRS * PNO, ORB))
            proj_h[n], proj_l[n] = split(dot3(flat, (block_h[n], block_l[n]), NN))
            return 0

        lax.fori_loop(0, 4, project, 0)

        def pair(p, _):
            rows = pl.ds(pl.multiple_of(p * PNO, PNO), PNO)
            left = proj_h[:, rows, :].reshape(4 * PNO, ORB), proj_l[:, rows, :].reshape(4 * PNO, ORB)
            both = dot3(left, (bases_h[p], bases_l[p]), NT)
            n = group * PAIRS + p
            for k in range(2):
                to = pl.ds((j * 2 + k) * PNO, PNO)
                f0_h[n, to, :], f0_l[n, to, :] = split(both[k * PNO : (k + 1) * PNO] * rates[p, stop * 2 + k])
            right = jnp.concatenate([both[2 * PNO : 3 * PNO], both[3 * PNO :]], axis=1)
            f1_h[n, :, pl.ds(j * 128, 128)], f1_l[n, :, pl.ds(j * 128, 128)] = split(right)
            return 0

        lax.fori_loop(0, PAIRS, pair, 0, unroll=4)

    def load_blocks(j):
        for n in range(4):
            m, k = n // 2, n % 2
            rows = [slots[j, a, b, k, m] for a in range(2) for b in range(2)]
            block_h[n], block_l[n] = split(jnp.concatenate(rows, axis=0))

    dress(0)
    fy(0).wait_recv()
    fy(1).wait_recv()
    for i in range(4):
        z_up(i).wait_recv()
        if i < SHIFT:
            relay_up(i).start()
        else:

            @pl.when(y == 0)
            def _():
                relay_up(i).start()

        z_down(4 + i).wait_recv()
        relay_down(4 + i).start()
        send_rows(1, (i,))

    @pl.when(zl == 1)
    def _():
        first_slot(1)

    send_stage(3)
    wts.start()
    bases.start()
    send_stage(2)
    for i in (3, 2, 1, 0):
        z_down(i).wait_recv()
        if i >= SHIFT:

            @pl.when(y > 0)
            def _():
                relay_down(i).start()

    to_twin(0).wait_recv()
    pltpu.make_async_copy(whole.at[0], slots.at[0, :, core], local_sem.at[1]).wait()
    load_blocks(0)
    fit(0, 0)
    for i in range(4):
        z_up(4 + i).wait_recv()
    readers(1, z1)
    readers(3, z3)
    for dx in (1, 3):
        for i in range(4):
            fx(dx, 0, i).wait_recv()
        to_twin(dx).start()
    dress(1)
    give_back(1)
    for dx in (2,):
        for i in range(4):
            fx(dx, 0, i).wait_recv()
        to_twin(dx).start()
    wts.wait_recv()
    rates_in = pltpu.make_async_copy(partner_weights, partner_rates, local_sem.at[1])
    rates_in.start()
    to_twin(1).wait_recv()
    rates_in.wait()
    bases.wait_recv()

    def split_other(p, _):
        other_h[p], other_l[p] = split(partner_bases[p])
        return 0

    lax.fori_loop(0, PAIRS, split_other, 0)
    fit(0, 1)
    load_blocks(1)
    fit(1, 0)
    fit(1, 1)
    dress(3)
    give_back(3)
    for i in range(8):
        relay_up(i).wait_recv()
    readers(2, z2)
    to_twin(3).wait_recv()
    load_blocks(3)
    fit(3, 0)
    fit(3, 1)
    dress(2)
    give_back(2)
    to_twin(2).wait_recv()
    load_blocks(2)
    fit(2, 0)
    fit(2, 1)

    def gather_terms(p, _):
        dressed[p] = natural(packed[p, PNO:, :]) + part(0, p)
        return 0

    lax.fori_loop(0, PAIRS, gather_terms, 0, unroll=4)
    for dz in (1, 3, 2):
        back[dz].wait_recv()

    def gather_parts(q, _):
        two = z_part[1, q] + z_part[2, q] + z_part[3, q]
        dressed[q] = dressed[q] + two[:, :PNO]
        dressed[q + 4] = dressed[q + 4] + two[:, PNO:]
        return 0

    lax.fori_loop(0, 4, gather_parts, 0, unroll=4)
    for q in range(4):
        d_send[q] = jnp.concatenate([dressed[q], dressed[q + 4]], axis=1)
    ds = [copy(DSEND[q], d_send.at[q], d_recv.at[q], partner) for q in range(4)]
    ps = [copy(PSEND[q], part_send.at[q], part_recv.at[q], partner) for q in range(4)]
    for q in range(4):
        ds[q].start()

    def fitted_sum(n, d):
        left = dot3((f0_h[n], f0_l[n]), split(d), NN)
        left = jnp.concatenate(
            [jnp.concatenate([left[i * PNO : (i + 1) * PNO], left[(i + 1) * PNO : (i + 2) * PNO]], axis=1) for i in (0, 2, 4, 6)],
            axis=1,
        )
        return dot3(split(left), (f1_h[n], f1_l[n]), NT)

    def finish_own(p, _):
        dressed[p] = dressed[p] + fitted_sum(p, dressed[p])
        return 0

    lax.fori_loop(0, PAIRS, finish_own, 0, unroll=8)
    for q in range(4):
        ds[q].wait_recv()
        two = d_recv[q]
        part_send[q] = jnp.concatenate(
            [fitted_sum(PAIRS + q, two[:, :PNO]), fitted_sum(PAIRS + q + 4, two[:, PNO:])], axis=1
        )
        ps[q].start()

    for done in (sh, bases, wts, *ds, *tabs.values(), *scls.values(), *back.values()):
        done.wait_send()

    @pl.when(turns == 1)
    def _():
        aside(0).wait_send()
        aside(1).wait_send()

    @pl.when(turns == 0)
    def _():
        fy(0).wait_send()
        fy(1).wait_send()

    @pl.when(bends == 1)
    def _():
        onward(0).wait_send()
        onward(1).wait_send()

    for i in range(8):
        z_up(i).wait_send()
        z_down(i).wait_send()
        relay_up(i).wait_send()
    for dx in (1, 2, 3):
        for i in range(4):
            fx(dx, 0, i).wait_send()
    for j in range(4):
        to_twin(j).wait_send()

    def plane_sent(n, _):
        @pl.when(lax.rem(n, 16) > 0)
        def _():
            plane_copy(lax.div(n, 16), lax.rem(n, 16)).wait_send()

        return 0

    lax.fori_loop(0, SLOTS, plane_sent, 0)
    for q in range(4):
        ps[q].wait()
        two = part_recv[q]
        out_ref[q] = dressed[q] + two[:, :PNO]
        out_ref[q + 4] = dressed[q + 4] + two[:, PNO:]


def on_device(pno_basis, amplitudes, send_list, couple, couple_weight, fit_weight, fit_blocks):
    zh, y, x, zl, _ = place()
    quarters = amplitudes.reshape(PAIRS, 4, 16, PNO).transpose(0, 2, 1, 3).reshape(PAIRS, 16, ORB)
    packed = jnp.concatenate([pno_basis, quarters], axis=1)

    t = jnp.arange(SLOTS, dtype=jnp.int32)
    source = ((zh + 4 - t // 16) % 4) * 16 + ((y + 4 - (t // 4) % 4) % 4) * 4 + (x + 4 - t % 4) % 4
    term = jnp.arange(PAIRS, dtype=jnp.int32)[:, None] * 8 + jnp.arange(8, dtype=jnp.int32)[None, :]
    inverse = jnp.sum(jnp.where(couple[None] == source[:, None, None], term[None], 0), axis=(1, 2))
    sends = send_list.reshape(SLOTS)
    table = jnp.concatenate(
        [jnp.pad(couple, ((0, 0), (0, 120))), jnp.broadcast_to(jnp.pad(inverse.reshape(1, SLOTS), ((0, 0), (0, 64))), (8, 128))]
    )
    scales = jnp.pad(couple_weight, ((0, 0), (0, 120)))
    weights = jnp.pad(fit_weight, ((0, 0), (0, 112)))

    vmem, smem = pl.BlockSpec(memory_space=pltpu.VMEM), pl.BlockSpec(memory_space=pltpu.SMEM)
    tile = functools.partial(pltpu.VMEM, dtype=F32)
    narrow = functools.partial(pltpu.VMEM, dtype=BF)
    out = pl.pallas_call(
        kernel,
        out_shape=jax.ShapeDtypeStruct((PAIRS, PNO, PNO), F32),
        in_specs=[smem] * 5 + [vmem] * 5,
        out_specs=vmem,
        scratch_shapes=[
            tile((PAIRS, PNO, ORB)), tile((PAIRS, PNO, ORB)), tile((PAIRS, PNO, ORB)),
            tile((2, 2, 2, PNO, ORB)),
            pltpu.VMEM((4, 16, 128), jnp.int32), pltpu.SMEM((4, 16, 128), jnp.int32),
            tile((4, 8, 128)), pltpu.SMEM((4, 8, 128), F32), tile((4, 4, PNO, 128)), tile((4, 4, PNO, 128)),
            tile((SLOTS, ROWS, ORB)), tile((SLOTS, ROWS, ORB)),
            tile((2, 2, 2, 2, PNO, ORB)), tile((4, 2, 2, 2, 2, PNO, ORB)),
            tile((PAIRS, PNO, ORB)), tile((PAIRS, 128)), pltpu.SMEM((PAIRS, 128), F32),
            narrow((4, PAIRS, PNO, ORB)), narrow((4, PAIRS, PNO, ORB)), narrow((PAIRS, PNO, ORB)), narrow((PAIRS, PNO, ORB)),
            narrow((4, ORB, ORB)), narrow((4, ORB, ORB)),
            narrow((4, PAIRS * PNO, ORB)), narrow((4, PAIRS * PNO, ORB)),
            narrow((16, 512, PNO)), narrow((16, 512, PNO)), narrow((16, PNO, 512)), narrow((16, PNO, 512)),
            tile((SLOTS, PNO, PNO)), tile((PAIRS, PNO, PNO)),
            tile((4, PNO, 128)), tile((4, PNO, 128)), tile((4, PNO, 128)), tile((4, PNO, 128)),
            pltpu.SemaphoreType.DMA((SLOTS,)), pltpu.SemaphoreType.DMA((SLOTS,)),
            pltpu.SemaphoreType.DMA((TRANSFERS,)), pltpu.SemaphoreType.DMA((TRANSFERS,)),
            pltpu.SemaphoreType.DMA((5,)),
        ],
        compiler_params=pltpu.CompilerParams(
            collective_id=0, has_side_effects=True, vmem_limit_bytes=60 * 1024 * 1024
        ),
    )(sends, inverse, couple, couple_weight, fit_weight, packed, fit_blocks, weights, table, scales)
    return out.reshape(PAIRS, PNO * PNO)


def solution(mesh):
    placed = (
        P(("blk", "dom"), None, None),
        P(("blk", "dom"), None),
        P("blk", "dom", None, None),
        P(("blk", "dom"), None),
        P(("blk", "dom"), None),
        P(("blk", "dom"), None),
        P("blk", None, "dom", None),
    )
    return jax.shard_map(
        on_device, mesh=mesh, in_specs=placed, out_specs=P(("blk", "dom"), None), check_vma=False
    )
```
